32 devices in a mesh: tm: 8 (over z, x), sta: 4 (over y, core).
Axes of the slice: x: 2, y: 2, z: 4, core: 2. Of those that a mesh axis runs over, the one named last changes fastest.
Arguments:
- data: bfloat16 [288, 16384], P('sta', 'tm'), may hold values from -6 to 6
- bank: bfloat16 [8, 288, 1024], P('tm', 'sta'), may hold values from -6 to 6
- select: int32 [4], replicated, may hold values from 0 to 7
- shifts: int32 [4, 288], P(None, 'sta'), may hold values from 0 to 255
Outputs:
- detection: float32 [4, 16384], P('sta', 'tm')
The draws below stay inside these ranges and needn't reach their ends.
All inputs are finite; a program needn't handle non-finite values. Where the reference program divides by a largest or mean magnitude, that divisor is 1e-20 or more.
Results may differ from the reference program's by a relative error of at most 0.0029.
Values may be sent and summed in bfloat16 or wider, within the bound.
No kernel may reach another device: no remote copies, remote signals or barrier semaphores. Data moves between devices by JAX's collectives and lax.ppermute only.
A program may use at most 64 MiB of HBM per device.

```python
import jax
import jax.numpy as jnp
from jax import lax

CH = 288
TL = 1024
K = 4
MAXSHIFT = 256
TIME = 16384
BANK = 8


def set_ends(drawn, stream_key, least, high):
    extent = drawn.shape
    index_at = [jax.random.randint(jax.random.fold_in(stream_key, axis), (), 0, extent[axis]) for axis in range(len(extent))]
    drawn = drawn.at[tuple(index_at)].set(least)
    longest = extent.index(max(extent))
    index_at[longest] = (index_at[longest] + 1) % extent[longest]
    return drawn.at[tuple(index_at)].set(high)


def level_of(own_key, dims, pieces, low, top_value):
    loudness = 1.0
    for axis_at, blocks in pieces:
        draws = jax.random.uniform(jax.random.fold_in(jax.random.fold_in(own_key, 6), axis_at), (blocks,), jnp.float32, low / len(pieces), top_value / len(pieces))
        loudness = loudness * jnp.repeat(jnp.exp(draws), dims[axis_at] // blocks).reshape((-1,) + (1,) * (len(dims) - 1 - axis_at))
    return loudness


def normal_values(key, shape, spread, bound, pieces=(), held_as=jnp.bfloat16):
    array = jax.random.normal(key, shape, jnp.float32) * spread
    if len(pieces) > 0:
        array = level_of(key, shape, pieces, -0.22, 0.18) * array
    return jnp.clip(array, min=-bound, max=bound).astype(held_as)


def setup_inputs(seed: int = 0) -> dict:
    seeds = jax.random.split(jax.random.key(seed), 5)
    return {
        "data": normal_values(seeds[0], (CH, TIME), 1.0, 6.0, ((0, 4), (1, 8))),
        "bank": normal_values(seeds[1], (BANK, CH, TL), 1.0, 6.0, ((0, 8), (1, 4))),
        "select": set_ends(jax.random.randint(seeds[2], (K,), 0, BANK), jax.random.fold_in(seeds[2], 1), 0, BANK - 1).astype(jnp.int32),
        "shifts": set_ends(jax.random.randint(seeds[3], (K, CH), 0, MAXSHIFT), jax.random.fold_in(seeds[3], 1), 0, MAXSHIFT - 1).astype(jnp.int32),
    }


def window_sums(values, out_length):
    width = 32
    span = TL // width
    nblocks = (out_length + TL) // width
    starts = out_length // width
    lead = values.shape[:-1]
    blocks = values[..., :nblocks * width].reshape(lead + (nblocks, width))
    inner_sums = jnp.cumsum(blocks, axis=-1) - blocks
    block_totals = lax.optimization_barrier(jnp.sum(blocks, axis=-1))
    running = jnp.concatenate([jnp.zeros(lead + (1,), jnp.float32), jnp.cumsum(block_totals, axis=-1)], axis=-1)
    whole_span = running[..., span:span + starts] - running[..., :starts]
    result = whole_span[..., None] - inner_sums[..., :starts, :] + inner_sums[..., span:span + starts, :]
    return result.reshape(lead + (out_length,))

def normalize_templates(rows):
    centred = rows - lax.optimization_barrier(jnp.mean(rows, axis=-1, keepdims=True))
    factor = lax.rsqrt(lax.optimization_barrier(jnp.sum(centred * centred, axis=-1, keepdims=True)) + 1e-05)
    return (centred * factor).astype(jnp.bfloat16)

def reference(data, bank, select, shifts):
    chosen = bank[select]
    templates_n = normalize_templates(chosen.astype(jnp.float32))
    extended = jnp.pad(data.astype(jnp.float32), ((0, 0), (0, TL + MAXSHIFT)))
    out_length = TIME + MAXSHIFT
    window_sum = window_sums(extended, out_length)
    window_sq = window_sums(extended * extended, out_length)
    scale_rows = lax.rsqrt(jnp.maximum(window_sq - window_sum * window_sum / TL, TL / 8.0))
    fft_length = 1 << (extended.shape[1] - 1).bit_length()
    spectrum = jnp.fft.rfft(extended, fft_length, axis=1)

    def one_template(paired):
        rows, offsets = paired
        tspec = jnp.fft.rfft(rows.astype(jnp.float32), fft_length, axis=1)
        correl = jnp.fft.irfft(spectrum * jnp.conj(tspec), fft_length, axis=1)[:, :out_length]
        normed = correl * scale_rows
        moved = jax.vmap(lambda series, offset: lax.dynamic_slice_in_dim(series, offset, TIME))(normed, offsets)
        return lax.optimization_barrier(jnp.sum(moved, axis=0))
    stacks = lax.map(one_template, (templates_n, shifts))
    peaks = lax.optimization_barrier(jnp.max(jnp.abs(stacks), axis=1, keepdims=True))
    return stacks / (peaks + 1e-06)
```

```python
import functools

import jax
import jax.numpy as jnp
from jax import lax
from jax.experimental import pallas as pl
from jax.experimental.pallas import tpu as pltpu
from jax.sharding import PartitionSpec as P

TL = 1024
MAXSHIFT = 256
LANES = 128
TPL_ROWS = TL // LANES
SHIFT_ROWS = MAXSHIFT // LANES
CHUNKS = TPL_ROWS + SHIFT_ROWS + 1
PAD_ROWS = 16
TILE_ROWS = 128


def partner(index, step, count):
    return index ^ step if count & (count - 1) == 0 else (index + step) % count


def source_of(index, step, count):
    return index ^ step if count & (count - 1) == 0 else (index - step + count) % count


def exchange(value, axis, step):
    count = lax.axis_size(axis)
    return lax.ppermute(value, axis, [(i, partner(i, step, count)) for i in range(count)])


def correlate_kernel(dims, me_ref, select_ref, shifts_ref, *refs):
    count, per, held, seg_rows, templates = dims
    blocks = refs[:count]
    out_ref, rows_ref, scale_ref, tot_ref, bank_ref, norm_ref, turn_ref, lag_ref, win_ref, raw_ref = refs[count:]
    rows = seg_rows * count
    me = me_ref[0]
    data_rows = per * seg_rows
    bank_rows = per * TPL_ROWS

    rows_ref[:, pl.ds(rows, PAD_ROWS), :] = jnp.zeros((per, PAD_ROWS, LANES), jnp.float32)
    for step in range(count):
        source = source_of(me, step, count)
        start = pl.multiple_of(source * seg_rows, seg_rows)
        part = blocks[step][pl.ds(0, data_rows), :].astype(jnp.float32)
        rows_ref[:, pl.ds(start, seg_rows), :] = part.reshape(per, seg_rows, LANES)
        part = blocks[step][pl.ds(data_rows, held * bank_rows), :].astype(jnp.float32)
        bank_ref[pl.ds(source * held, held)] = part.reshape(held, bank_rows, LANES)

    chosen = jnp.concatenate([bank_ref[pl.ds(select_ref[k], 1)] for k in range(templates)], 0)
    chosen = chosen.reshape(templates, per, TPL_ROWS, LANES)
    mean = jnp.sum(jnp.sum(chosen, 2, keepdims=True), 3, keepdims=True) * (1.0 / TL)
    centred = chosen - mean
    power = jnp.sum(jnp.sum(centred * centred, 2, keepdims=True), 3, keepdims=True)
    normed = centred * lax.rsqrt(power + 1e-05)
    norm_ref[...] = normed.astype(jnp.bfloat16).astype(jnp.float32)

    lane = lax.broadcasted_iota(jnp.int32, (LANES, 2 * LANES), 1)
    depth = lax.broadcasted_iota(jnp.int32, (LANES, 2 * LANES), 0)
    summing = jnp.where(lane <= depth, 1.0, jnp.where(lane >= LANES, 1.0, 0.0)).astype(jnp.bfloat16)
    out_ref[...] = jnp.zeros_like(out_ref)

    def window(values, slot):
        ends = tot_ref.at[slot]
        need = rows + 8
        got = [jnp.dot(v, summing, preferred_element_type=jnp.float32) for v in values]
        got = functools.reduce(jnp.add, got)
        tail, whole = got[:, :LANES], got[:, LANES:]
        ends[pl.ds(0, rows + PAD_ROWS), :] = whole
        ends[pl.ds(rows + PAD_ROWS, 8), :] = jnp.zeros((8, LANES), jnp.float32)
        for reach in (1, 2, 4):
            extent = rows + PAD_ROWS
            summed = ends[pl.ds(0, extent), :] + ends[pl.ds(reach, extent), :]
            ends[pl.ds(0, extent), :] = summed
        return tail[:need] - tail[8 : need + 8] + ends[pl.ds(1, need), :]

    def channel(c, carry):
        series = rows_ref[c]
        squared = series * series
        high = squared.astype(jnp.bfloat16)
        low = (squared - high.astype(jnp.float32)).astype(jnp.bfloat16)
        window_sum = window([series.astype(jnp.bfloat16)], 0)
        window_sq = window([high, low], 1)
        scale = lax.rsqrt(jnp.maximum(window_sq - window_sum * window_sum * (1.0 / TL), TL / 8.0))
        scale_ref[pl.ds(0, rows + 8), :] = scale

        for k in range(templates):
            shift = shifts_ref[k, me * per + c]
            whole, part = shift // LANES, shift % LANES
            turn_ref[k] = pltpu.roll(norm_ref[k, c], part, 1)
            for quarter in range(4):
                base = part + 32 * quarter
                lanes = lax.broadcasted_iota(jnp.int32, (32, LANES), 1)
                moved_by = lax.broadcasted_iota(jnp.int32, (32, LANES), 0) + base
                first = lanes >= moved_by
                second = lanes >= moved_by - LANES
                zero = jnp.zeros((32, LANES), jnp.float32)
                older, old = zero, zero
                place = pl.ds(k * LANES + 32 * quarter, 32)
                for p in range(CHUNKS - 1):
                    if p < TPL_ROWS:
                        row = jnp.broadcast_to(turn_ref[k, pl.ds(p, 1), :], (32, LANES))
                        now = pltpu.roll(row, 32 * quarter, 1, stride=1, stride_axis=0)
                    else:
                        now = zero
                    piece = jnp.where(first, now, jnp.where(second, old, older))
                    at = pl.multiple_of((p + whole) * LANES, LANES)
                    lag_ref[place, pl.ds(at, LANES)] = piece.astype(jnp.bfloat16)
                    older, old = old, now
                rest = pl.multiple_of(jnp.where(whole == 0, CHUNKS - 1, 0) * LANES, LANES)
                lag_ref[place, pl.ds(rest, LANES)] = jnp.zeros((32, LANES), jnp.bfloat16)

        def tile(i, carry):
            top = pl.multiple_of(i * tile_rows, tile_rows)
            for q in range(CHUNKS):
                piece = rows_ref[c, pl.ds(top + q, tile_rows), :]
                win_ref[:, pl.ds(q * LANES, LANES)] = piece.astype(jnp.bfloat16)
            raw_ref[...] = lax.dot_general(
                win_ref[...], lag_ref[...], (((1,), (1,)), ((), ())), preferred_element_type=jnp.float32
            )
            for k in range(templates):
                shift = shifts_ref[k, me * per + c]
                whole, part = shift // LANES, shift % LANES
                here = scale_ref[pl.ds(top + whole, tile_rows), :]
                after = scale_ref[pl.ds(top + whole + 1, tile_rows), :]
                lanes = lax.broadcasted_iota(jnp.int32, (tile_rows, LANES), 1)
                mixed = jnp.where(lanes >= part, here, after)
                moved = pltpu.roll(mixed, LANES - part, 1)
                out_ref[k, pl.ds(top, tile_rows), :] += raw_ref[:, pl.ds(k * LANES, LANES)] * moved
            return carry

        tile_rows = min(TILE_ROWS, rows)
        if rows == tile_rows:
            tile(0, 0)
        else:
            lax.fori_loop(0, rows // tile_rows, tile, 0)
        return carry

    lax.fori_loop(0, per, channel, 0)


def correlate(blocks, me, select, shifts, per, held, seg_rows):
    count = len(blocks)
    templates = select.shape[0]
    rows = seg_rows * count
    tile_rows = min(TILE_ROWS, rows)
    smem = pl.BlockSpec(memory_space=pltpu.SMEM)
    vmem = pl.BlockSpec(memory_space=pltpu.VMEM)
    f32, bf16 = jnp.float32, jnp.bfloat16
    macs = per * rows * CHUNKS * LANES * templates * LANES
    return pl.pallas_call(
        functools.partial(correlate_kernel, (count, per, held, seg_rows, templates)),
        out_shape=jax.ShapeDtypeStruct((templates, rows, LANES), f32),
        in_specs=[smem, smem, smem] + [vmem] * count,
        out_specs=vmem,
        scratch_shapes=[
            pltpu.VMEM((per, rows + PAD_ROWS, LANES), f32),
            pltpu.VMEM((rows + PAD_ROWS, LANES), f32),
            pltpu.VMEM((2, rows + PAD_ROWS + 8, LANES), f32),
            pltpu.VMEM((count * held, per * TPL_ROWS, LANES), f32),
            pltpu.VMEM((templates, per, TPL_ROWS, LANES), f32),
            pltpu.VMEM((templates, TPL_ROWS, LANES), f32),
            pltpu.VMEM((templates * LANES, CHUNKS * LANES), bf16),
            pltpu.VMEM((tile_rows, CHUNKS * LANES), bf16),
            pltpu.VMEM((tile_rows, templates * LANES), f32),
        ],
        compiler_params=pltpu.CompilerParams(vmem_limit_bytes=48 << 20),
        cost_estimate=pl.CostEstimate(flops=2 * macs, bytes_accessed=1 << 20, transcendentals=0),
    )(me, select, shifts, *blocks)


def on_device(data, bank, select, shifts):
    channels, samples = data.shape
    templates = select.shape[0]
    held = bank.shape[0]
    count = lax.axis_size("tm")
    stations = lax.axis_size("sta")
    me = lax.axis_index("tm")
    seg_rows = samples // LANES
    per = -(-channels // count)
    spare = per * count - channels
    if spare:
        data = jnp.pad(data, ((0, spare), (0, 0)))
        bank = jnp.pad(bank, ((0, 0), (0, spare), (0, 0)))
        shifts = jnp.pad(shifts, ((0, 0), (0, spare)))

    wave_rows = data.reshape(count, per * seg_rows, LANES)
    bank_rows = bank.reshape(held, count, per * TPL_ROWS, LANES).transpose(1, 0, 2, 3)
    bank_rows = bank_rows.reshape(count, held * per * TPL_ROWS, LANES)
    outgoing = jnp.concatenate([wave_rows, bank_rows], axis=1)
    blocks = [lax.dynamic_index_in_dim(outgoing, me, 0, keepdims=False)]
    for step in range(1, count):
        there = partner(me, step, count)
        block = lax.dynamic_index_in_dim(outgoing, there, 0, keepdims=False)
        blocks.append(exchange(block, "tm", step))
    stacks = correlate(blocks, me.reshape(1), select, shifts, per, held, seg_rows)

    mine = lax.axis_index("sta")
    stacks = stacks.reshape(stations, templates // stations, seg_rows * count, LANES)
    summed = lax.dynamic_index_in_dim(stacks, mine, 0, keepdims=False)
    for step in range(1, stations):
        there = partner(mine, step, stations)
        part = lax.dynamic_index_in_dim(stacks, there, 0, keepdims=False)
        summed = summed + exchange(part, "sta", step)
    if count & (count - 1) == 0:
        step = 1
        while step < count:
            summed = summed + exchange(summed, "tm", step)
            step *= 2
    else:
        summed = lax.psum(summed, "tm")
    peaks = jnp.max(jnp.abs(summed), axis=(1, 2), keepdims=True)
    segment = lax.dynamic_slice_in_dim(summed, me * seg_rows, seg_rows, 1)
    return (segment / (peaks + 1e-06)).reshape(templates // stations, samples)


def solution(mesh):
    in_specs = (P("sta", "tm"), P("tm", "sta", None), P(), P(None, "sta"))
    out_specs = P("sta", "tm")
    return jax.shard_map(
        on_device, mesh=mesh, in_specs=in_specs, out_specs=out_specs, check_vma=False
    )
```

```python
import functools

import jax
import jax.numpy as jnp
from jax import lax
from jax.experimental import pallas as pl
from jax.experimental.pallas import tpu as pltpu
from jax.sharding import PartitionSpec as P

TL = 1024
MAXSHIFT = 256
LANES = 128
TPL_ROWS = TL // LANES
CHUNKS = TPL_ROWS + 1
LAG_ROWS = 8
PAD_ROWS = 16
TILE_ROWS = 128


def exchange(value, axis, step):
    count = lax.axis_size(axis)
    return lax.ppermute(value, axis, [(i, i ^ step) for i in range(count)])


def passed_on(value, axis, step):
    count = lax.axis_size(axis)
    return lax.ppermute(value, axis, [(i, (i + step) % count) for i in range(count)])


def correlate_kernel(dims, me_ref, select_ref, shifts_ref, *refs):
    count, per, held, seg_rows, templates = dims
    blocks = refs[:count]
    out_ref, rows_ref, scale_a, scale_b, tot_ref, bank_ref, norm_ref, lag_a, lag_b, win_ref, raw_ref = refs[count:]
    rows = seg_rows * count
    tile_rows = min(TILE_ROWS, rows)
    me = me_ref[0]
    data_rows = per * seg_rows
    bank_rows = per * TPL_ROWS

    rows_ref[:, pl.ds(rows, PAD_ROWS), :] = jnp.zeros((per, PAD_ROWS, LANES), jnp.float32)
    for step in range(count):
        source = lax.rem(me - step + count, count)
        start = pl.multiple_of(source * seg_rows, seg_rows)
        part = blocks[step][pl.ds(0, data_rows), :].astype(jnp.float32)
        rows_ref[:, pl.ds(start, seg_rows), :] = part.reshape(per, seg_rows, LANES)
        part = blocks[step][pl.ds(data_rows, held * bank_rows), :].astype(jnp.float32)
        bank_ref[pl.ds(source * held, held)] = part.reshape(held, bank_rows, LANES)

    chosen = jnp.concatenate([bank_ref[pl.ds(select_ref[k], 1)] for k in range(templates)], 0)
    chosen = chosen.reshape(templates, per, TPL_ROWS, LANES)
    mean = jnp.sum(jnp.sum(chosen, 2, keepdims=True), 3, keepdims=True) * (1.0 / TL)
    centred = chosen - mean
    power = jnp.sum(jnp.sum(centred * centred, 2, keepdims=True), 3, keepdims=True)
    normed = centred * lax.rsqrt(power + 1e-05)
    norm_ref[...] = normed.astype(jnp.bfloat16).astype(jnp.float32)

    lane = lax.broadcasted_iota(jnp.int32, (LANES, 2 * LANES), 1)
    depth = lax.broadcasted_iota(jnp.int32, (LANES, 2 * LANES), 0)
    summing = jnp.where(lane <= depth, 1.0, jnp.where(lane >= LANES, 1.0, 0.0)).astype(jnp.bfloat16)
    out_ref[...] = jnp.zeros_like(out_ref)

    def window(values, slot):
        ends = tot_ref.at[slot]
        need = rows + 8
        got = [jnp.dot(v, summing, preferred_element_type=jnp.float32) for v in values]
        got = functools.reduce(jnp.add, got)
        tail, whole = got[:, :LANES], got[:, LANES:]
        ends[pl.ds(0, rows + PAD_ROWS), :] = whole
        ends[pl.ds(rows + PAD_ROWS, 8), :] = jnp.zeros((8, LANES), jnp.float32)
        for reach in (1, 2, 4):
            extent = rows + PAD_ROWS
            summed = ends[pl.ds(0, extent), :] + ends[pl.ds(reach, extent), :]
            ends[pl.ds(0, extent), :] = summed
        return tail[:need] - tail[8 : need + 8] + ends[pl.ds(1, need), :]

    step_lane = lax.broadcasted_iota(jnp.int32, (LAG_ROWS, LANES), 1)
    step_row = lax.broadcasted_iota(jnp.int32, (LAG_ROWS, LANES), 0)

    def prepare(c, scale_ref, lag_ref):
        series = rows_ref[c]
        squared = series * series
        high = squared.astype(jnp.bfloat16)
        low = (squared - high.astype(jnp.float32)).astype(jnp.bfloat16)
        window_sum = window([series.astype(jnp.bfloat16)], 0)
        window_sq = window([high, low], 1)
        scale = lax.rsqrt(jnp.maximum(window_sq - window_sum * window_sum * (1.0 / TL), TL / 8.0))
        scale_ref[...] = scale
        for k in range(templates):
            spread = [
                jnp.broadcast_to(norm_ref[k, c, pl.ds(p, 1), :], (LAG_ROWS, LANES))
                for p in range(TPL_ROWS)
            ]
            for group in range(LANES // LAG_ROWS):
                ahead = step_lane >= step_row + group * LAG_ROWS
                turned = [
                    pltpu.roll(row, group * LAG_ROWS, 1, stride=1, stride_axis=0) for row in spread
                ]
                zero = jnp.zeros((LAG_ROWS, LANES), jnp.float32)
                pieces = [
                    jnp.where(ahead, now, old) for now, old in zip(turned + [zero], [zero] + turned)
                ]
                place = pl.ds(k * LANES + group * LAG_ROWS, LAG_ROWS)
                lag_ref[place, :] = jnp.concatenate(pieces, 1).astype(jnp.bfloat16)

    def accumulate(c, scale_ref, lag_ref):
        def tile(top):
            for q in range(0, CHUNKS, 2):
                both = range(q, min(q + 2, CHUNKS))
                pieces = [rows_ref[c, pl.ds(top + p, tile_rows + 8), :] for p in both]
                place = pl.ds(q * LANES, len(both) * LANES)
                win_ref[:, place] = jnp.concatenate(pieces, 1).astype(jnp.bfloat16)
            raw = lax.dot_general(
                win_ref[...], lag_ref[...], (((1,), (1,)), ((), ())), preferred_element_type=jnp.float32
            )
            scale = scale_ref[pl.ds(top, tile_rows + 8), :]
            for k in range(templates):
                raw_ref[k] = raw[:, k * LANES : (k + 1) * LANES] * scale
            for k in range(templates):
                shift = shifts_ref[k, me * per + c]
                whole, part = shift // LANES, shift % LANES
                here = raw_ref[k, pl.ds(whole, tile_rows), :]
                after = raw_ref[k, pl.ds(whole + 1, tile_rows), :]
                lanes = lax.broadcasted_iota(jnp.int32, (tile_rows, LANES), 1)
                mixed = jnp.where(lanes >= part, here, after)
                moved = pltpu.roll(mixed, LANES - part, 1)
                out_ref[k, pl.ds(top, tile_rows), :] += moved

        if rows == tile_rows:
            tile(0)
        else:
            pl.loop(0, rows // tile_rows)(lambda i: tile(pl.multiple_of(i * tile_rows, tile_rows)))

    first, second = (scale_a, lag_a), (scale_b, lag_b)
    prepare(0, *first)

    def pair(i):
        prepare(2 * i + 1, *second)
        accumulate(2 * i, *first)
        prepare(jnp.minimum(2 * i + 2, per - 1), *first)
        accumulate(2 * i + 1, *second)

    pl.loop(0, per // 2)(pair)
    if per % 2:
        accumulate(per - 1, *first)


def correlate(blocks, me, select, shifts, per, held, seg_rows):
    count = len(blocks)
    templates = select.shape[0]
    rows = seg_rows * count
    tile_rows = min(TILE_ROWS, rows)
    smem = pl.BlockSpec(memory_space=pltpu.SMEM)
    vmem = pl.BlockSpec(memory_space=pltpu.VMEM)
    f32, bf16 = jnp.float32, jnp.bfloat16
    macs = per * rows * CHUNKS * LANES * templates * LANES
    return pl.pallas_call(
        functools.partial(correlate_kernel, (count, per, held, seg_rows, templates)),
        out_shape=jax.ShapeDtypeStruct((templates, rows, LANES), f32),
        in_specs=[smem, smem, smem] + [vmem] * count,
        out_specs=vmem,
        scratch_shapes=[
            pltpu.VMEM((per, rows + PAD_ROWS, LANES), f32),
            pltpu.VMEM((rows + 8, LANES), f32),
            pltpu.VMEM((rows + 8, LANES), f32),
            pltpu.VMEM((2, rows + PAD_ROWS + 8, LANES), f32),
            pltpu.VMEM((count * held, per * TPL_ROWS, LANES), f32),
            pltpu.VMEM((templates, per, TPL_ROWS, LANES), f32),
            pltpu.VMEM((templates * LANES, CHUNKS * LANES), bf16),
            pltpu.VMEM((templates * LANES, CHUNKS * LANES), bf16),
            pltpu.VMEM((tile_rows + 8, CHUNKS * LANES), bf16),
            pltpu.VMEM((templates, tile_rows + 8, LANES), f32),
        ],
        compiler_params=pltpu.CompilerParams(vmem_limit_bytes=48 << 20),
        cost_estimate=pl.CostEstimate(flops=2 * macs, bytes_accessed=1 << 20, transcendentals=0),
    )(me, select, shifts, *blocks)


def on_device(data, bank, select, shifts):
    channels, samples = data.shape
    templates = select.shape[0]
    held = bank.shape[0]
    count = lax.axis_size("tm")
    stations = lax.axis_size("sta")
    me = lax.axis_index("tm")
    seg_rows = samples // LANES
    per = -(-channels // count)
    spare = per * count - channels
    if spare:
        data = jnp.pad(data, ((0, spare), (0, 0)))
        bank = jnp.pad(bank, ((0, 0), (0, spare), (0, 0)))
        shifts = jnp.pad(shifts, ((0, 0), (0, spare)))

    wave_rows = data.reshape(count, per * seg_rows, LANES)
    bank_rows = bank.reshape(held, count, per * TPL_ROWS, LANES).transpose(1, 0, 2, 3)
    bank_rows = bank_rows.reshape(count, held * per * TPL_ROWS, LANES)
    outgoing = jnp.concatenate([wave_rows, bank_rows], axis=1)
    blocks = [lax.dynamic_index_in_dim(outgoing, me, 0, keepdims=False)]
    for step in range(1, count):
        there = lax.rem(me + step, count)
        block = lax.dynamic_index_in_dim(outgoing, there, 0, keepdims=False)
        blocks.append(passed_on(block, "tm", step))
    stacks = correlate(blocks, me.reshape(1), select, shifts, per, held, seg_rows)

    mine = lax.axis_index("sta")
    stacks = stacks.reshape(stations, templates // stations, seg_rows * count, LANES)
    summed = lax.dynamic_index_in_dim(stacks, mine, 0, keepdims=False)
    for step in range(1, stations):
        there = lax.rem(mine + step, stations)
        part = lax.dynamic_index_in_dim(stacks, there, 0, keepdims=False)
        summed = summed + passed_on(part, "sta", step)
    if count & (count - 1) == 0:
        step = 1
        while step < count:
            summed = summed + exchange(summed, "tm", step)
            step *= 2
    else:
        summed = lax.psum(summed, "tm")
    peaks = jnp.max(jnp.abs(summed), axis=(1, 2), keepdims=True)
    segment = lax.dynamic_slice_in_dim(summed, me * seg_rows, seg_rows, 1)
    return (segment / (peaks + 1e-06)).reshape(templates // stations, samples)


def solution(mesh):
    in_specs = (P("sta", "tm"), P("tm", "sta", None), P(), P(None, "sta"))
    out_specs = P("sta", "tm")
    return jax.shard_map(
        on_device, mesh=mesh, in_specs=in_specs, out_specs=out_specs, check_vma=False
    )
```

```python
import functools

import jax
import jax.numpy as jnp
from jax import lax
from jax.experimental import pallas as pl
from jax.experimental.pallas import tpu as pltpu
from jax.sharding import PartitionSpec as P

TL = 1024
MAXSHIFT = 256
LANES = 128
TPL_ROWS = TL // LANES
CHUNKS = TPL_ROWS + 1
LAG_ROWS = 8
HALF = LANES // 2
PACK_VMEM = 67043328
PAD_ROWS = 24
TILE_ROWS = 128


def exchange(value, axis, step):
    count = lax.axis_size(axis)
    return lax.ppermute(value, axis, [(i, i ^ step) for i in range(count)])


def passed_on(value, axis, step):
    count = lax.axis_size(axis)
    return lax.ppermute(value, axis, [(i, (i + step) % count) for i in range(count)])


def pack_kernel(dims, me_ref, select_hbm, shifts_hbm, data_hbm, bank_hbm, *refs):
    count, per, held, seg_rows, templates = dims
    blocks, table_ref = refs[:count], refs[count]
    select_ref, shifts_ref, data_ref, bank_ref, wave_ref, tpl_ref, sems = refs[count + 1 :]
    pairs = [
        (bank_hbm, bank_ref),
        (data_hbm, data_ref),
        (select_hbm, select_ref),
        (shifts_hbm, shifts_ref),
    ]
    fetch = [pltpu.make_async_copy(a, b, sems.at[i]) for i, (a, b) in enumerate(pairs)]
    for copy in fetch:
        copy.start()
    me = me_ref[0]
    fetch[0].wait()
    for e in range(held):
        for q in range(TPL_ROWS):
            piece = bank_ref[e, :, pl.ds(q * LANES, LANES)].astype(jnp.float32)
            tpl_ref[pl.ds(q, count * per, stride=TPL_ROWS), :] = piece
        for i in range(count):
            start = pl.multiple_of(lax.rem(me + i, count) * (per * TPL_ROWS), TPL_ROWS)
            part = tpl_ref[pl.ds(start, per * TPL_ROWS), :]
            place = pl.ds(per * seg_rows + e * per * TPL_ROWS, per * TPL_ROWS)
            blocks[i][place, :] = part.astype(jnp.bfloat16)
    fetch[1].wait()
    for r in range(seg_rows):
        piece = data_ref[:, pl.ds(r * LANES, LANES)].astype(jnp.float32)
        wave_ref[pl.ds(r, count * per, stride=seg_rows), :] = piece
    for i in range(count):
        start = pl.multiple_of(lax.rem(me + i, count) * (per * seg_rows), 8)
        part = wave_ref[pl.ds(start, per * seg_rows), :]
        blocks[i][pl.ds(0, per * seg_rows), :] = part.astype(jnp.bfloat16)
    fetch[2].wait()
    fetch[3].wait()
    for k in range(templates):
        table_ref[k] = select_ref[k]
        for c in range(per):
            table_ref[templates * (c + 1) + k] = shifts_ref[k, me * per + c]


def pack(me, select, shifts, data, bank, count):
    channels, samples = data.shape
    held = bank.shape[0]
    per, seg_rows = channels // count, samples // LANES
    hbm = pl.BlockSpec(memory_space=pltpu.MemorySpace.HBM)
    vmem = pl.BlockSpec(memory_space=pltpu.VMEM)
    smem = pl.BlockSpec(memory_space=pltpu.SMEM)
    templates = select.shape[0]
    block = jax.ShapeDtypeStruct((per * (seg_rows + held * TPL_ROWS), LANES), jnp.bfloat16)
    return pl.pallas_call(
        functools.partial(pack_kernel, (count, per, held, seg_rows, templates)),
        out_shape=[block] * count + [jax.ShapeDtypeStruct((templates * (per + 1),), jnp.int32)],
        in_specs=[smem] + [hbm] * 4,
        out_specs=[vmem] * count + [smem],
        scratch_shapes=[
            pltpu.SMEM(select.shape, jnp.int32),
            pltpu.SMEM(shifts.shape, jnp.int32),
            pltpu.VMEM(data.shape, jnp.bfloat16),
            pltpu.VMEM(bank.shape, jnp.bfloat16),
            pltpu.VMEM((channels * seg_rows, LANES), jnp.float32),
            pltpu.VMEM((channels * TPL_ROWS, LANES), jnp.float32),
            pltpu.SemaphoreType.DMA((4,)),
        ],
        compiler_params=pltpu.CompilerParams(vmem_limit_bytes=PACK_VMEM),
    )(me, select, shifts, data, bank)


def finish_kernel(seg_rows, me_ref, *refs):
    parts, out_ref = refs[:-1], refs[-1]
    start = pl.multiple_of(me_ref[0] * seg_rows, seg_rows)
    for j in range(out_ref.shape[0]):
        total = functools.reduce(jnp.add, [part[j] for part in parts])
        peak = jnp.max(jnp.max(jnp.abs(total), 0, keepdims=True), 1, keepdims=True)
        segment = functools.reduce(jnp.add, [part[j, pl.ds(start, seg_rows), :] for part in parts])
        segment = segment / (peak + 1e-06)
        for r in range(seg_rows):
            out_ref[pl.ds(j, 1), pl.ds(r * LANES, LANES)] = segment[r : r + 1]


def finish(parts, me, seg_rows):
    smem = pl.BlockSpec(memory_space=pltpu.SMEM)
    vmem = pl.BlockSpec(memory_space=pltpu.VMEM)
    return pl.pallas_call(
        functools.partial(finish_kernel, seg_rows),
        out_shape=jax.ShapeDtypeStruct((parts[0].shape[0], seg_rows * LANES), jnp.float32),
        in_specs=[smem] + [vmem] * len(parts),
        out_specs=vmem,
        compiler_params=pltpu.CompilerParams(vmem_limit_bytes=24 << 20),
    )(me, *parts)


def correlate_kernel(dims, me_ref, table_ref, *refs):
    count, per, held, seg_rows, templates = dims
    blocks = refs[:count]
    out_ref, rows_ref, scale_a, scale_b, tot_ref, bank_ref, norm_ref, lag_a, lag_b, win_ref, half_ref, raw_ref = refs[count:]
    rows = seg_rows * count
    tile_rows = min(TILE_ROWS, rows)
    height = tile_rows + 8
    me = me_ref[0]
    data_rows = per * seg_rows
    bank_rows = per * TPL_ROWS

    rows_ref[:, pl.ds(rows, PAD_ROWS), :] = jnp.zeros((per, PAD_ROWS, LANES), jnp.float32)
    for step in range(count):
        source = lax.rem(me - step + count, count)
        start = pl.multiple_of(source * seg_rows, seg_rows)
        part = blocks[step][pl.ds(0, data_rows), :].astype(jnp.float32)
        rows_ref[:, pl.ds(start, seg_rows), :] = part.reshape(per, seg_rows, LANES)
        part = blocks[step][pl.ds(data_rows, held * bank_rows), :].astype(jnp.float32)
        bank_ref[pl.ds(source * held, held)] = part.reshape(held, bank_rows, LANES)

    chosen = jnp.concatenate([bank_ref[pl.ds(table_ref[k], 1)] for k in range(templates)], 0)
    chosen = chosen.reshape(templates, per, TPL_ROWS, LANES)
    mean = jnp.sum(jnp.sum(chosen, 2, keepdims=True), 3, keepdims=True) * (1.0 / TL)
    centred = chosen - mean
    power = jnp.sum(jnp.sum(centred * centred, 2, keepdims=True), 3, keepdims=True)
    normed = centred * lax.rsqrt(power + 1e-05)
    norm_ref[...] = normed.astype(jnp.bfloat16).astype(jnp.float32)

    lane = lax.broadcasted_iota(jnp.int32, (LANES, 2 * LANES), 1)
    depth = lax.broadcasted_iota(jnp.int32, (LANES, 2 * LANES), 0)
    summing = jnp.where(lane <= depth, 1.0, jnp.where(lane >= LANES, 1.0, 0.0)).astype(jnp.bfloat16)
    out_ref[...] = jnp.zeros_like(out_ref)

    def window(values, slot):
        ends = tot_ref.at[slot]
        need, extent = rows + 8, rows + 16
        got = [jnp.dot(v, summing, preferred_element_type=jnp.float32) for v in values]
        got = functools.reduce(jnp.add, got)
        tail, whole = got[:, :LANES], got[:, LANES:]
        ends[pl.ds(0, extent), :] = whole
        ends[pl.ds(extent, 8), :] = jnp.zeros((8, LANES), jnp.float32)
        for reach in (1, 2, 4):
            summed = ends[pl.ds(0, extent), :] + ends[pl.ds(reach, extent), :]
            ends[pl.ds(0, extent), :] = summed
        return tail[:need] - tail[8 : need + 8] + ends[pl.ds(1, need), :]

    step_lane = lax.broadcasted_iota(jnp.int32, (LAG_ROWS, LANES), 1)
    step_row = lax.broadcasted_iota(jnp.int32, (LAG_ROWS, LANES), 0)

    def prepare(c, scale_ref, lag_ref):
        series = rows_ref[c, pl.ds(0, rows + 16), :]
        squared = series * series
        high = squared.astype(jnp.bfloat16)
        low = (squared - high.astype(jnp.float32)).astype(jnp.bfloat16)
        window_sum = window([series.astype(jnp.bfloat16)], 0)
        window_sq = window([high, low], 1)
        scale = lax.rsqrt(jnp.maximum(window_sq - window_sum * window_sum * (1.0 / TL), TL / 8.0))
        scale_ref[...] = scale
        for k in range(templates):
            spread = [
                jnp.broadcast_to(norm_ref[k, c, pl.ds(p, 1), :], (LAG_ROWS, LANES))
                for p in range(TPL_ROWS)
            ]
            for group in range(HALF // LAG_ROWS):
                ahead = step_lane >= step_row + group * LAG_ROWS
                turned = [
                    pltpu.roll(row, group * LAG_ROWS, 1, stride=1, stride_axis=0) for row in spread
                ]
                zero = jnp.zeros((LAG_ROWS, LANES), jnp.float32)
                pieces = [
                    jnp.where(ahead, now, old) for now, old in zip(turned + [zero], [zero] + turned)
                ]
                place = pl.ds(k * HALF + group * LAG_ROWS, LAG_ROWS)
                lag_ref[place, :] = jnp.concatenate(pieces, 1).astype(jnp.bfloat16)

    def accumulate(c, scale_ref, lag_ref):
        def tile(top):
            span = tile_rows + 16
            before = rows_ref[c, pl.ds(top, span), :]
            behind = rows_ref[c, pl.ds(top + 1, span), :]
            late = lax.broadcasted_iota(jnp.int32, (span, LANES), 1) >= HALF
            half_ref[...] = pltpu.roll(jnp.where(late, before, behind), HALF, 1)
            for q in range(0, CHUNKS, 2):
                both = range(q, min(q + 2, CHUNKS))
                place = pl.ds(q * LANES, len(both) * LANES)
                pieces = [rows_ref[c, pl.ds(top + p, height), :] for p in both]
                win_ref[pl.ds(0, height), place] = jnp.concatenate(pieces, 1).astype(jnp.bfloat16)
                pieces = [half_ref[pl.ds(p, height), :] for p in both]
                win_ref[pl.ds(height, height), place] = jnp.concatenate(pieces, 1).astype(jnp.bfloat16)
            raw = lax.dot_general(
                win_ref[...], lag_ref[...], (((1,), (1,)), ((), ())), preferred_element_type=jnp.float32
            )
            scale = scale_ref[pl.ds(top, height), :]
            late = lax.broadcasted_iota(jnp.int32, (height, LANES), 1) >= HALF
            for k in range(0, templates, 2):
                low = raw[:height, k * HALF : k * HALF + LANES]
                high = raw[height:, k * HALF : k * HALF + LANES]
                raw_ref[k] = jnp.where(late, pltpu.roll(high, HALF, 1), low) * scale
                raw_ref[k + 1] = jnp.where(late, high, pltpu.roll(low, HALF, 1)) * scale
            for k in range(templates):
                shift = table_ref[templates * (c + 1) + k]
                whole, part = shift // LANES, shift % LANES
                here = raw_ref[k, pl.ds(whole, tile_rows), :]
                after = raw_ref[k, pl.ds(whole + 1, tile_rows), :]
                lanes = lax.broadcasted_iota(jnp.int32, (tile_rows, LANES), 1)
                mixed = jnp.where(lanes >= part, here, after)
                moved = pltpu.roll(mixed, LANES - part, 1)
                out_ref[k, pl.ds(top, tile_rows), :] += moved

        if rows == tile_rows:
            tile(0)
        else:
            pl.loop(0, rows // tile_rows)(lambda i: tile(pl.multiple_of(i * tile_rows, tile_rows)))

    first, second = (scale_a, lag_a), (scale_b, lag_b)
    prepare(0, *first)

    def pair(i):
        prepare(2 * i + 1, *second)
        accumulate(2 * i, *first)
        prepare(jnp.minimum(2 * i + 2, per - 1), *first)
        accumulate(2 * i + 1, *second)

    pl.loop(0, per // 2)(pair)
    if per % 2:
        accumulate(per - 1, *first)


def correlate(blocks, me, table, templates, per, held, seg_rows):
    count = len(blocks)
    rows = seg_rows * count
    tile_rows = min(TILE_ROWS, rows)
    smem = pl.BlockSpec(memory_space=pltpu.SMEM)
    vmem = pl.BlockSpec(memory_space=pltpu.VMEM)
    f32, bf16 = jnp.float32, jnp.bfloat16
    macs = per * rows * CHUNKS * LANES * templates * LANES
    return pl.pallas_call(
        functools.partial(correlate_kernel, (count, per, held, seg_rows, templates)),
        out_shape=jax.ShapeDtypeStruct((templates, rows, LANES), f32),
        in_specs=[smem, smem] + [vmem] * count,
        out_specs=vmem,
        scratch_shapes=[
            pltpu.VMEM((per, rows + PAD_ROWS, LANES), f32),
            pltpu.VMEM((rows + 8, LANES), f32),
            pltpu.VMEM((rows + 8, LANES), f32),
            pltpu.VMEM((2, rows + PAD_ROWS, LANES), f32),
            pltpu.VMEM((count * held, per * TPL_ROWS, LANES), f32),
            pltpu.VMEM((templates, per, TPL_ROWS, LANES), f32),
            pltpu.VMEM((templates * HALF, CHUNKS * LANES), bf16),
            pltpu.VMEM((templates * HALF, CHUNKS * LANES), bf16),
            pltpu.VMEM((2 * (tile_rows + 8), CHUNKS * LANES), bf16),
            pltpu.VMEM((tile_rows + 16, LANES), f32),
            pltpu.VMEM((templates, tile_rows + 8, LANES), f32),
        ],
        compiler_params=pltpu.CompilerParams(vmem_limit_bytes=48 << 20),
        cost_estimate=pl.CostEstimate(flops=2 * macs, bytes_accessed=1 << 20, transcendentals=0),
    )(me, table, *blocks)


def on_device(data, bank, select, shifts):
    channels, samples = data.shape
    templates = select.shape[0]
    held = bank.shape[0]
    count = lax.axis_size("tm")
    stations = lax.axis_size("sta")
    me = lax.axis_index("tm")
    seg_rows = samples // LANES
    per = -(-channels // count)
    spare = per * count - channels
    if spare:
        data = jnp.pad(data, ((0, spare), (0, 0)))
        bank = jnp.pad(bank, ((0, 0), (0, spare), (0, 0)))
        shifts = jnp.pad(shifts, ((0, 0), (0, spare)))

    packed = pack(me.reshape(1), select, shifts, data, bank, count)
    blocks, table = list(packed[:count]), packed[count]
    for step in range(1, count):
        blocks[step] = passed_on(blocks[step], "tm", step)
    stacks = correlate(blocks, me.reshape(1), table, templates, per, held, seg_rows)

    mine = lax.axis_index("sta")
    stacks = stacks.reshape(stations, templates // stations, seg_rows * count, LANES)
    summed = lax.dynamic_index_in_dim(stacks, mine, 0, keepdims=False)
    for step in range(1, stations):
        there = lax.rem(mine + step, stations)
        part = lax.dynamic_index_in_dim(stacks, there, 0, keepdims=False)
        summed = summed + passed_on(part, "sta", step)
    parts, step = [summed], 1
    while step < count:
        radix = 2 if (count // step).bit_length() % 2 == 0 else 4
        summed = functools.reduce(jnp.add, parts)
        parts = [summed] + [exchange(summed, "tm", step * turn) for turn in range(1, radix)]
        step *= radix
    return finish(parts, me.reshape(1), seg_rows)


def solution(mesh):
    in_specs = (P("sta", "tm"), P("tm", "sta", None), P(), P(None, "sta"))
    out_specs = P("sta", "tm")
    return jax.shard_map(
        on_device, mesh=mesh, in_specs=in_specs, out_specs=out_specs, check_vma=False
    )
```

```python
import functools

import jax
import jax.numpy as jnp
from jax import lax
from jax.experimental import pallas as pl
from jax.experimental.pallas import tpu as pltpu
from jax.sharding import PartitionSpec as P

TL = 1024
MAXSHIFT = 256
LANES = 128
TPL_ROWS = TL // LANES
SHIFT_ROWS = MAXSHIFT // LANES
GROUP = 8
BEYOND = SHIFT_ROWS + TPL_ROWS + 1
CHUNKS = TPL_ROWS + 1
LAG_ROWS = 8
HALF = LANES // 2
PACK_VMEM = 24 << 20


def exchange(value, axis, step):
    count = lax.axis_size(axis)
    return lax.ppermute(value, axis, [(i, i ^ step) for i in range(count)])


def passed_on(value, axis, step):
    count = lax.axis_size(axis)
    return lax.ppermute(value, axis, [(i, (i + step) % count) for i in range(count)])


def pack_kernel(dims, me_ref, select_hbm, shifts_hbm, data_hbm, bank_hbm, *refs):
    count, per, held, seg_rows, templates = dims
    blocks, table_ref = refs[:count], refs[count]
    select_ref, shifts_ref, data_ref, bank_ref, wave_ref, tpl_ref, sems = refs[count + 1 :]
    pairs = [
        (bank_hbm, bank_ref),
        (data_hbm, data_ref),
        (select_hbm, select_ref),
        (shifts_hbm, shifts_ref),
    ]
    fetch = [pltpu.make_async_copy(a, b, sems.at[i]) for i, (a, b) in enumerate(pairs)]
    for copy in fetch:
        copy.start()
    me = me_ref[0]
    fetch[0].wait()
    for e in range(held):
        for q in range(TPL_ROWS):
            piece = bank_ref[e, :, pl.ds(q * LANES, LANES)].astype(jnp.float32)
            tpl_ref[pl.ds(q, count * per, stride=TPL_ROWS), :] = piece
        for i in range(count):
            start = pl.multiple_of(lax.rem(me + i, count) * (per * TPL_ROWS), TPL_ROWS)
            part = tpl_ref[pl.ds(start, per * TPL_ROWS), :]
            place = pl.ds(per * seg_rows + e * per * TPL_ROWS, per * TPL_ROWS)
            blocks[i][place, :] = part.astype(jnp.bfloat16)
    fetch[1].wait()
    for r in range(seg_rows):
        piece = data_ref[:, pl.ds(r * LANES, LANES)].astype(jnp.float32)
        wave_ref[pl.ds(r, count * per, stride=seg_rows), :] = piece
    for i in range(count):
        start = pl.multiple_of(lax.rem(me + i, count) * (per * seg_rows), 8)
        part = wave_ref[pl.ds(start, per * seg_rows), :]
        blocks[i][pl.ds(0, per * seg_rows), :] = part.astype(jnp.bfloat16)
    fetch[2].wait()
    fetch[3].wait()
    for k in range(templates):
        table_ref[k] = select_ref[k]
        for c in range(per):
            table_ref[templates * (c + 1) + k] = shifts_ref[k, me * per + c]


def pack(me, select, shifts, data, bank, count):
    channels, samples = data.shape
    held = bank.shape[0]
    per, seg_rows = channels // count, samples // LANES
    hbm = pl.BlockSpec(memory_space=pltpu.MemorySpace.HBM)
    vmem = pl.BlockSpec(memory_space=pltpu.VMEM)
    smem = pl.BlockSpec(memory_space=pltpu.SMEM)
    templates = select.shape[0]
    block = jax.ShapeDtypeStruct((per * (seg_rows + held * TPL_ROWS), LANES), jnp.bfloat16)
    return pl.pallas_call(
        functools.partial(pack_kernel, (count, per, held, seg_rows, templates)),
        out_shape=[block] * count + [jax.ShapeDtypeStruct((templates * (per + 1),), jnp.int32)],
        in_specs=[smem] + [hbm] * 4,
        out_specs=[vmem] * count + [smem],
        scratch_shapes=[
            pltpu.SMEM(select.shape, jnp.int32),
            pltpu.SMEM(shifts.shape, jnp.int32),
            pltpu.VMEM(data.shape, jnp.bfloat16),
            pltpu.VMEM(bank.shape, jnp.bfloat16),
            pltpu.VMEM((channels * seg_rows, LANES), jnp.float32),
            pltpu.VMEM((channels * TPL_ROWS, LANES), jnp.float32),
            pltpu.SemaphoreType.DMA((4,)),
        ],
        compiler_params=pltpu.CompilerParams(vmem_limit_bytes=PACK_VMEM),
    )(me, *[pltpu.with_memory_space_constraint(v, pltpu.MemorySpace.HBM) for v in (select, shifts, data, bank)])


def finish_kernel(seg_rows, me_ref, *refs):
    parts, out_ref = refs[:-1], refs[-1]
    me = me_ref[0]
    start = (me // GROUP) * (seg_rows * GROUP) + me % GROUP
    for j in range(out_ref.shape[0]):
        total = functools.reduce(jnp.add, [part[j] for part in parts])
        peak = jnp.max(jnp.max(jnp.abs(total), 0, keepdims=True), 1, keepdims=True)
        rows = [part[j, pl.ds(start, seg_rows, stride=GROUP), :] for part in parts]
        segment = functools.reduce(jnp.add, rows) / (peak + 1e-06)
        for r in range(seg_rows):
            out_ref[pl.ds(j, 1), pl.ds(r * LANES, LANES)] = segment[r : r + 1]


def finish(parts, me, seg_rows):
    smem = pl.BlockSpec(memory_space=pltpu.SMEM)
    vmem = pl.BlockSpec(memory_space=pltpu.VMEM)
    return pl.pallas_call(
        functools.partial(finish_kernel, seg_rows),
        out_shape=jax.ShapeDtypeStruct((parts[0].shape[0], seg_rows * LANES), jnp.float32),
        in_specs=[smem] + [vmem] * len(parts),
        out_specs=vmem,
        compiler_params=pltpu.CompilerParams(vmem_limit_bytes=24 << 20),
    )(me, *parts)


def correlate_kernel(dims, me_ref, table_ref, *refs):
    count, per, held, seg_rows, templates = dims
    blocks = refs[:count]
    out_ref, rows_ref, bank_ref, norm_ref, lag_a, lag_b, *more = refs[count:]
    win_a, win_b, late_a, late_b, raw_a, raw_b = more
    groups = count // GROUP
    tiles = seg_rows + BEYOND
    block_rows = seg_rows * GROUP
    starts = (seg_rows + SHIFT_ROWS) * GROUP
    paired = starts + (TPL_ROWS - 1) * GROUP
    me = me_ref[0]
    data_rows = per * seg_rows
    bank_rows = per * TPL_ROWS

    for step in range(count):
        source = lax.rem(me - step + count, count)
        before = lax.rem(source - 1 + count, count)
        part = blocks[step][pl.ds(0, data_rows), :].astype(jnp.float32)
        for c in range(per):
            piece = part[c * seg_rows : (c + 1) * seg_rows]
            at = (c * groups + source // GROUP) * (tiles * GROUP) + source % GROUP
            rows_ref[pl.ds(at, seg_rows, stride=GROUP), :] = piece
            piece = jnp.where(source > 0, piece[:BEYOND], 0.0)
            at = (c * groups + before // GROUP) * (tiles * GROUP) + before % GROUP
            rows_ref[pl.ds(at + block_rows, BEYOND, stride=GROUP), :] = piece
        part = blocks[step][pl.ds(data_rows, held * bank_rows), :].astype(jnp.float32)
        bank_ref[pl.ds(source * held, held)] = part.reshape(held, bank_rows, LANES)

    chosen = jnp.concatenate([bank_ref[pl.ds(table_ref[k], 1)] for k in range(templates)], 0)
    chosen = chosen.reshape(templates, per, TPL_ROWS, LANES)
    mean = jnp.sum(jnp.sum(chosen, 2, keepdims=True), 3, keepdims=True) * (1.0 / TL)
    centred = chosen - mean
    power = jnp.sum(jnp.sum(centred * centred, 2, keepdims=True), 3, keepdims=True)
    normed = centred * lax.rsqrt(power + 1e-05)
    norm_ref[...] = normed.astype(jnp.bfloat16).astype(jnp.float32)

    lane = lax.broadcasted_iota(jnp.int32, (LANES, 2 * LANES), 1)
    depth = lax.broadcasted_iota(jnp.int32, (LANES, 2 * LANES), 0)
    summing = jnp.where(lane <= depth, 1.0, jnp.where(lane >= LANES, 1.0, 0.0)).astype(jnp.bfloat16)
    summing_twice = jnp.concatenate([summing, summing], 0)

    def window(values, weights):
        got = jnp.dot(values, weights, preferred_element_type=jnp.float32)
        tail, total = got[:, :LANES], got[:, LANES:]
        for reach in (1, 2, 4):
            extent = total.shape[0] - reach * GROUP
            total = total[:extent] + total[reach * GROUP :]
        far = TPL_ROWS * GROUP
        return tail[:starts] - tail[far : far + starts] + total[GROUP : GROUP + starts]

    step_lane = lax.broadcasted_iota(jnp.int32, (LAG_ROWS, LANES), 1)
    step_row = lax.broadcasted_iota(jnp.int32, (LAG_ROWS, LANES), 0)

    def prepare(c, lag_ref):
        for k in range(templates):
            spread = [
                jnp.broadcast_to(norm_ref[k, c, pl.ds(p, 1), :], (LAG_ROWS, LANES))
                for p in range(TPL_ROWS)
            ]
            for group in range(HALF // LAG_ROWS):
                ahead = step_lane >= step_row + group * LAG_ROWS
                turned = [
                    pltpu.roll(row, group * LAG_ROWS, 1, stride=1, stride_axis=0) for row in spread
                ]
                zero = jnp.zeros((LAG_ROWS, LANES), jnp.float32)
                pieces = [
                    jnp.where(ahead, now, old) for now, old in zip(turned + [zero], [zero] + turned)
                ]
                place = pl.ds(k * HALF + group * LAG_ROWS, LAG_ROWS)
                lag_ref[place, :] = jnp.concatenate(pieces, 1).astype(jnp.bfloat16)

    def accumulate(c, first, lag_ref, win_ref, late_ref, raw_ref):
        def group(g):
            base = pl.multiple_of((c * groups + g) * (tiles * GROUP), GROUP)
            series = rows_ref[pl.ds(base, tiles * GROUP), :]

            heard = series[: starts + TPL_ROWS * GROUP]
            squared = heard * heard
            high = squared.astype(jnp.bfloat16)
            low = (squared - high.astype(jnp.float32)).astype(jnp.bfloat16)
            window_sum = window(heard.astype(jnp.bfloat16), summing)
            window_sq = window(jnp.concatenate([high, low], 1), summing_twice)
            spread = window_sq - window_sum * window_sum * (1.0 / TL)
            scale = lax.rsqrt(jnp.maximum(spread, TL / 8.0))

            extent = paired + GROUP
            latter = lax.broadcasted_iota(jnp.int32, (extent, LANES), 1) >= HALF
            later = jnp.where(latter, series[:extent], series[GROUP : GROUP + extent])
            later = pltpu.roll(later, HALF, 1)
            for ref, values in ((win_ref, series), (late_ref, later)):
                both = [values[:paired], values[GROUP : GROUP + paired]]
                ref[...] = jnp.concatenate(both, 1).astype(jnp.bfloat16)

            def windows(ref):
                pieces = [ref[pl.ds(q * GROUP, starts), :] for q in range(0, TPL_ROWS, 2)]
                pieces.append(ref[pl.ds(paired - starts, starts), pl.ds(LANES, LANES)])
                return jnp.concatenate(pieces, 1)

            raw = lax.dot_general(
                jnp.concatenate([windows(win_ref), windows(late_ref)], 0),
                lag_ref[...],
                (((1,), (1,)), ((), ())),
                preferred_element_type=jnp.float32,
            )
            latter = lax.broadcasted_iota(jnp.int32, (starts, LANES), 1) >= HALF
            for k in range(0, templates, 2):
                early = raw[:starts, k * HALF : k * HALF + LANES]
                late = raw[starts:, k * HALF : k * HALF + LANES]
                kept = jnp.where(latter, late, early)
                swapped = pltpu.roll(jnp.where(latter, early, late), HALF, 1)
                raw_ref[k] = jnp.where(latter, swapped, kept) * scale
                raw_ref[k + 1] = jnp.where(latter, kept, swapped) * scale
            lanes = lax.broadcasted_iota(jnp.int32, (block_rows, LANES), 1)
            for k in range(templates):
                shift = table_ref[templates * (c + 1) + k]
                whole, part = shift // LANES, shift % LANES
                at = pl.multiple_of(whole * GROUP, GROUP)
                here = raw_ref[k, pl.ds(at, block_rows), :]
                after = raw_ref[k, pl.ds(at + GROUP, block_rows), :]
                moved = pltpu.roll(jnp.where(lanes >= part, here, after), LANES - part, 1)
                place = pl.ds(pl.multiple_of(g * block_rows, block_rows), block_rows)
                if first:
                    out_ref[k, place, :] = moved
                else:
                    out_ref[k, place, :] += moved

        if groups == 1:
            group(0)
        else:
            pl.loop(0, groups)(group)

    buffers = [(lag_a, win_a, late_a, raw_a), (lag_b, win_b, late_b, raw_b)]
    prepare(0, lag_a)
    for c in range(per):
        if c + 1 < per:
            prepare(c + 1, buffers[(c + 1) % 2][0])
        accumulate(c, c == 0, *buffers[c % 2])


def correlate(blocks, me, table, templates, per, held, seg_rows):
    count = len(blocks)
    rows = seg_rows * count
    starts = (seg_rows + SHIFT_ROWS) * GROUP
    paired = starts + (TPL_ROWS - 1) * GROUP
    smem = pl.BlockSpec(memory_space=pltpu.SMEM)
    vmem = pl.BlockSpec(memory_space=pltpu.VMEM)
    f32, bf16 = jnp.float32, jnp.bfloat16
    macs = per * rows * CHUNKS * LANES * templates * LANES
    return pl.pallas_call(
        functools.partial(correlate_kernel, (count, per, held, seg_rows, templates)),
        out_shape=jax.ShapeDtypeStruct((templates, rows, LANES), f32),
        in_specs=[smem, smem] + [vmem] * count,
        out_specs=vmem,
        scratch_shapes=[
            pltpu.VMEM((per * count * (seg_rows + BEYOND) + GROUP * GROUP, LANES), f32),
            pltpu.VMEM((count * held, per * TPL_ROWS, LANES), f32),
            pltpu.VMEM((templates, per, TPL_ROWS, LANES), f32),
            *[pltpu.VMEM((templates * HALF, CHUNKS * LANES), bf16)] * 2,
            *[pltpu.VMEM((paired, 2 * LANES), bf16)] * 4,
            *[pltpu.VMEM((templates, starts, LANES), f32)] * 2,
        ],
        compiler_params=pltpu.CompilerParams(vmem_limit_bytes=48 << 20),
        cost_estimate=pl.CostEstimate(flops=2 * macs, bytes_accessed=1 << 20, transcendentals=0),
    )(me, table, *blocks)


def on_device(data, bank, select, shifts):
    channels, samples = data.shape
    templates = select.shape[0]
    held = bank.shape[0]
    count = lax.axis_size("tm")
    stations = lax.axis_size("sta")
    me = lax.axis_index("tm")
    seg_rows = samples // LANES
    per = -(-channels // count)
    spare = per * count - channels
    if spare:
        data = jnp.pad(data, ((0, spare), (0, 0)))
        bank = jnp.pad(bank, ((0, 0), (0, spare), (0, 0)))
        shifts = jnp.pad(shifts, ((0, 0), (0, spare)))

    packed = pack(me.reshape(1), select, shifts, data, bank, count)
    blocks, table = list(packed[:count]), packed[count]
    for step in range(1, count):
        blocks[step] = passed_on(blocks[step], "tm", step)
    stacks = correlate(blocks, me.reshape(1), table, templates, per, held, seg_rows)

    mine = lax.axis_index("sta")
    stacks = stacks.reshape(stations, templates // stations, seg_rows * count, LANES)
    summed = lax.dynamic_index_in_dim(stacks, mine, 0, keepdims=False)
    for step in range(1, stations):
        there = lax.rem(mine + step, stations)
        part = lax.dynamic_index_in_dim(stacks, there, 0, keepdims=False)
        summed = summed + passed_on(part, "sta", step)
    parts, step = [summed], 1
    while step < count:
        radix = 2 if (count // step).bit_length() % 2 == 0 else 4
        summed = functools.reduce(jnp.add, parts)
        parts = [summed] + [exchange(summed, "tm", step * turn) for turn in range(1, radix)]
        step *= radix
    return finish(parts, me.reshape(1), seg_rows)


def solution(mesh):
    in_specs = (P("sta", "tm"), P("tm", "sta", None), P(), P(None, "sta"))
    out_specs = P("sta", "tm")
    return jax.shard_map(
        on_device, mesh=mesh, in_specs=in_specs, out_specs=out_specs, check_vma=False
    )
```

```python
import functools

import jax
import jax.numpy as jnp
from jax import lax
from jax.experimental import pallas as pl
from jax.experimental.pallas import tpu as pltpu
from jax.sharding import PartitionSpec as P

TL = 1024
MAXSHIFT = 256
LANES = 128
TPL_ROWS = TL // LANES
SHIFT_ROWS = MAXSHIFT // LANES
GROUP = 8
BEYOND = SHIFT_ROWS + TPL_ROWS + 1
CHUNKS = TPL_ROWS + 1
LAG_ROWS = 8
HALF = LANES // 2
PACK_VMEM = 24 << 20


def exchange(value, axis, step):
    count = lax.axis_size(axis)
    return lax.ppermute(value, axis, [(i, i ^ step) for i in range(count)])


def visiting_order(count):
    half = max(count // 2, 1)
    far, near = range(count - 1, half - 1, -1), range(half - 1, 0, -1)
    order = [step for part in (far, near) for odd in (1, 0) for step in part if step % 2 == odd]
    return order


def passed_on(value, axis, step):
    count = lax.axis_size(axis)
    return lax.ppermute(value, axis, [(i, (i + step) % count) for i in range(count)])


def pack_kernel(dims, me_ref, select_hbm, shifts_hbm, data_hbm, bank_hbm, *refs):
    count, per, held, seg_rows, templates = dims
    blocks, table_ref = refs[:count], refs[count]
    select_ref, shifts_ref, data_ref, bank_ref, wave_ref, tpl_ref, sems = refs[count + 1 :]
    pairs = [
        (bank_hbm, bank_ref),
        (data_hbm, data_ref),
        (select_hbm, select_ref),
        (shifts_hbm, shifts_ref),
    ]
    fetch = [pltpu.make_async_copy(a, b, sems.at[i]) for i, (a, b) in enumerate(pairs)]
    for copy in fetch:
        copy.start()
    me = me_ref[0]
    fetch[0].wait()
    for e in range(held):
        for q in range(TPL_ROWS):
            piece = bank_ref[e, :, pl.ds(q * LANES, LANES)].astype(jnp.float32)
            tpl_ref[pl.ds(q, count * per, stride=TPL_ROWS), :] = piece
        for i in range(count):
            start = pl.multiple_of((me ^ i) * (per * TPL_ROWS), TPL_ROWS)
            part = tpl_ref[pl.ds(start, per * TPL_ROWS), :]
            place = pl.ds(per * seg_rows + e * per * TPL_ROWS, per * TPL_ROWS)
            blocks[i][place, :] = part.astype(jnp.bfloat16)
    fetch[1].wait()
    for r in range(seg_rows):
        piece = data_ref[:, pl.ds(r * LANES, LANES)].astype(jnp.float32)
        wave_ref[pl.ds(r, count * per, stride=seg_rows), :] = piece
    for i in range(count):
        start = pl.multiple_of((me ^ i) * (per * seg_rows), 8)
        part = wave_ref[pl.ds(start, per * seg_rows), :]
        blocks[i][pl.ds(0, per * seg_rows), :] = part.astype(jnp.bfloat16)
    fetch[2].wait()
    fetch[3].wait()
    for k in range(templates):
        table_ref[k] = select_ref[k]
        for c in range(per):
            table_ref[templates * (c + 1) + k] = shifts_ref[k, me * per + c]


def pack(me, select, shifts, data, bank, count):
    channels, samples = data.shape
    held = bank.shape[0]
    per, seg_rows = channels // count, samples // LANES
    hbm = pl.BlockSpec(memory_space=pltpu.MemorySpace.HBM)
    vmem = pl.BlockSpec(memory_space=pltpu.VMEM)
    smem = pl.BlockSpec(memory_space=pltpu.SMEM)
    templates = select.shape[0]
    block = jax.ShapeDtypeStruct((per * (seg_rows + held * TPL_ROWS), LANES), jnp.bfloat16)
    return pl.pallas_call(
        functools.partial(pack_kernel, (count, per, held, seg_rows, templates)),
        out_shape=[block] * count + [jax.ShapeDtypeStruct((templates * (per + 1),), jnp.int32)],
        in_specs=[smem] + [hbm] * 4,
        out_specs=[vmem] * count + [smem],
        scratch_shapes=[
            pltpu.SMEM(select.shape, jnp.int32),
            pltpu.SMEM(shifts.shape, jnp.int32),
            pltpu.VMEM(data.shape, jnp.bfloat16),
            pltpu.VMEM(bank.shape, jnp.bfloat16),
            pltpu.VMEM((channels * seg_rows, LANES), jnp.float32),
            pltpu.VMEM((channels * TPL_ROWS, LANES), jnp.float32),
            pltpu.SemaphoreType.DMA((4,)),
        ],
        compiler_params=pltpu.CompilerParams(vmem_limit_bytes=PACK_VMEM),
    )(me, *[pltpu.with_memory_space_constraint(v, pltpu.MemorySpace.HBM) for v in (select, shifts, data, bank)])


def finish_kernel(seg_rows, me_ref, *refs):
    parts, out_ref = refs[:-1], refs[-1]
    me = me_ref[0]
    start = (me // GROUP) * (seg_rows * GROUP) + me % GROUP
    for j in range(out_ref.shape[0]):
        total = functools.reduce(jnp.add, [part[j] for part in parts])
        peak = jnp.max(jnp.max(jnp.abs(total), 0, keepdims=True), 1, keepdims=True)
        rows = [part[j, pl.ds(start, seg_rows, stride=GROUP), :] for part in parts]
        segment = functools.reduce(jnp.add, rows) / (peak + 1e-06)
        for r in range(seg_rows):
            out_ref[pl.ds(j, 1), pl.ds(r * LANES, LANES)] = segment[r : r + 1]


def finish(parts, me, seg_rows):
    smem = pl.BlockSpec(memory_space=pltpu.SMEM)
    vmem = pl.BlockSpec(memory_space=pltpu.VMEM)
    return pl.pallas_call(
        functools.partial(finish_kernel, seg_rows),
        out_shape=jax.ShapeDtypeStruct((parts[0].shape[0], seg_rows * LANES), jnp.float32),
        in_specs=[smem] + [vmem] * len(parts),
        out_specs=vmem,
        compiler_params=pltpu.CompilerParams(vmem_limit_bytes=24 << 20),
    )(me, *parts)


def correlate_kernel(dims, steps, me_ref, table_vmem, *refs):
    count, per, held, seg_rows, templates = dims
    blocks = refs[:count]
    out_ref, rows_ref, bank_ref, norm_ref, lag_a, lag_b, *more = refs[count:]
    win_a, win_b, late_a, late_b, raw_a, raw_b, table_ref, sem = more
    fetch = pltpu.make_async_copy(table_vmem, table_ref, sem)
    fetch.start()
    groups = count // GROUP
    tiles = seg_rows + BEYOND
    block_rows = seg_rows * GROUP
    starts = (seg_rows + SHIFT_ROWS) * GROUP
    paired = starts + (TPL_ROWS - 1) * GROUP
    me = me_ref[0]
    data_rows = per * seg_rows
    bank_rows = per * TPL_ROWS

    for block, step in zip(blocks, steps):
        source = me ^ step
        before = lax.rem(source - 1 + count, count)
        part = block[pl.ds(0, data_rows), :].astype(jnp.float32)
        for c in range(per):
            piece = part[c * seg_rows : (c + 1) * seg_rows]
            at = (c * groups + source // GROUP) * (tiles * GROUP) + source % GROUP
            rows_ref[pl.ds(at, seg_rows, stride=GROUP), :] = piece
            piece = jnp.where(source > 0, piece[:BEYOND], 0.0)
            at = (c * groups + before // GROUP) * (tiles * GROUP) + before % GROUP
            rows_ref[pl.ds(at + block_rows, BEYOND, stride=GROUP), :] = piece
        part = block[pl.ds(data_rows, held * bank_rows), :].astype(jnp.float32)
        bank_ref[pl.ds(source * held, held)] = part.reshape(held, bank_rows, LANES)

    fetch.wait()

    chosen = jnp.concatenate([bank_ref[pl.ds(table_ref[k], 1)] for k in range(templates)], 0)
    chosen = chosen.reshape(templates, per, TPL_ROWS, LANES)
    mean = jnp.sum(jnp.sum(chosen, 2, keepdims=True), 3, keepdims=True) * (1.0 / TL)
    centred = chosen - mean
    power = jnp.sum(jnp.sum(centred * centred, 2, keepdims=True), 3, keepdims=True)
    normed = centred * lax.rsqrt(power + 1e-05)
    norm_ref[...] = normed.astype(jnp.bfloat16).astype(jnp.float32)

    lane = lax.broadcasted_iota(jnp.int32, (LANES, 2 * LANES), 1)
    depth = lax.broadcasted_iota(jnp.int32, (LANES, 2 * LANES), 0)
    summing = jnp.where(lane <= depth, 1.0, jnp.where(lane >= LANES, 1.0, 0.0)).astype(jnp.bfloat16)
    summing_twice = jnp.concatenate([summing, summing], 0)

    def window(values, weights):
        got = jnp.dot(values, weights, preferred_element_type=jnp.float32)
        tail, total = got[:, :LANES], got[:, LANES:]
        for reach in (1, 2, 4):
            extent = total.shape[0] - reach * GROUP
            total = total[:extent] + total[reach * GROUP :]
        far = TPL_ROWS * GROUP
        return tail[:starts] - tail[far : far + starts] + total[GROUP : GROUP + starts]

    step_lane = lax.broadcasted_iota(jnp.int32, (LAG_ROWS, LANES), 1)
    step_row = lax.broadcasted_iota(jnp.int32, (LAG_ROWS, LANES), 0)

    def prepare(c, lag_ref):
        for k in range(templates):
            spread = [
                jnp.broadcast_to(norm_ref[k, c, pl.ds(p, 1), :], (LAG_ROWS, LANES))
                for p in range(TPL_ROWS)
            ]
            for group in range(HALF // LAG_ROWS):
                ahead = step_lane >= step_row + group * LAG_ROWS
                turned = [
                    pltpu.roll(row, group * LAG_ROWS, 1, stride=1, stride_axis=0) for row in spread
                ]
                zero = jnp.zeros((LAG_ROWS, LANES), jnp.float32)
                pieces = [
                    jnp.where(ahead, now, old) for now, old in zip(turned + [zero], [zero] + turned)
                ]
                place = pl.ds(k * HALF + group * LAG_ROWS, LAG_ROWS)
                lag_ref[place, :] = jnp.concatenate(pieces, 1).astype(jnp.bfloat16)

    def accumulate(c, first, lag_ref, win_ref, late_ref, raw_ref):
        def group(g):
            base = pl.multiple_of((c * groups + g) * (tiles * GROUP), GROUP)
            series = rows_ref[pl.ds(base, tiles * GROUP), :]

            heard = series[: starts + TPL_ROWS * GROUP]
            squared = heard * heard
            high = squared.astype(jnp.bfloat16)
            low = (squared - high.astype(jnp.float32)).astype(jnp.bfloat16)
            window_sum = window(heard.astype(jnp.bfloat16), summing)
            window_sq = window(jnp.concatenate([high, low], 1), summing_twice)
            spread = window_sq - window_sum * window_sum * (1.0 / TL)
            scale = lax.rsqrt(jnp.maximum(spread, TL / 8.0))

            extent = paired + GROUP
            latter = lax.broadcasted_iota(jnp.int32, (extent, LANES), 1) >= HALF
            later = jnp.where(latter, series[:extent], series[GROUP : GROUP + extent])
            later = pltpu.roll(later, HALF, 1)
            for ref, values in ((win_ref, series), (late_ref, later)):
                both = [values[:paired], values[GROUP : GROUP + paired]]
                ref[...] = jnp.concatenate(both, 1).astype(jnp.bfloat16)

            def windows(ref):
                pieces = [ref[pl.ds(q * GROUP, starts), :] for q in range(0, TPL_ROWS, 2)]
                pieces.append(ref[pl.ds(paired - starts, starts), pl.ds(LANES, LANES)])
                return jnp.concatenate(pieces, 1)

            raw = lax.dot_general(
                jnp.concatenate([windows(win_ref), windows(late_ref)], 0),
                lag_ref[...],
                (((1,), (1,)), ((), ())),
                preferred_element_type=jnp.float32,
            )
            latter = lax.broadcasted_iota(jnp.int32, (starts, LANES), 1) >= HALF
            for k in range(0, templates, 2):
                early = raw[:starts, k * HALF : k * HALF + LANES]
                late = raw[starts:, k * HALF : k * HALF + LANES]
                kept = jnp.where(latter, late, early)
                swapped = pltpu.roll(jnp.where(latter, early, late), HALF, 1)
                raw_ref[k] = jnp.where(latter, swapped, kept) * scale
                raw_ref[k + 1] = jnp.where(latter, kept, swapped) * scale
            lanes = lax.broadcasted_iota(jnp.int32, (block_rows, LANES), 1)
            for k in range(templates):
                shift = table_ref[templates * (c + 1) + k]
                whole, part = shift // LANES, shift % LANES
                at = pl.multiple_of(whole * GROUP, GROUP)
                here = raw_ref[k, pl.ds(at, block_rows), :]
                after = raw_ref[k, pl.ds(at + GROUP, block_rows), :]
                moved = pltpu.roll(jnp.where(lanes >= part, here, after), LANES - part, 1)
                place = pl.ds(pl.multiple_of(g * block_rows, block_rows), block_rows)
                if first:
                    out_ref[k, place, :] = moved
                else:
                    out_ref[k, place, :] += moved

        if groups == 1:
            group(0)
        else:
            pl.loop(0, groups)(group)

    buffers = [(lag_a, win_a, late_a, raw_a), (lag_b, win_b, late_b, raw_b)]
    prepare(0, lag_a)
    for c in range(per):
        if c + 1 < per:
            prepare(c + 1, buffers[(c + 1) % 2][0])
        accumulate(c, c == 0, *buffers[c % 2])


def correlate(blocks, order, me, table, templates, per, held, seg_rows):
    count = len(blocks)
    rows = seg_rows * count
    starts = (seg_rows + SHIFT_ROWS) * GROUP
    paired = starts + (TPL_ROWS - 1) * GROUP
    smem = pl.BlockSpec(memory_space=pltpu.SMEM)
    vmem = pl.BlockSpec(memory_space=pltpu.VMEM)
    f32, bf16 = jnp.float32, jnp.bfloat16
    macs = per * rows * CHUNKS * LANES * templates * LANES
    return pl.pallas_call(
        functools.partial(correlate_kernel, (count, per, held, seg_rows, templates), [0] + order),
        out_shape=jax.ShapeDtypeStruct((templates, rows, LANES), f32),
        in_specs=[smem, vmem] + [vmem] * count,
        out_specs=vmem,
        scratch_shapes=[
            pltpu.VMEM((per * count * (seg_rows + BEYOND) + GROUP * GROUP, LANES), f32),
            pltpu.VMEM((count * held, per * TPL_ROWS, LANES), f32),
            pltpu.VMEM((templates, per, TPL_ROWS, LANES), f32),
            *[pltpu.VMEM((templates * HALF, CHUNKS * LANES), bf16)] * 2,
            *[pltpu.VMEM((paired, 2 * LANES), bf16)] * 4,
            *[pltpu.VMEM((templates, starts, LANES), f32)] * 2,
            pltpu.SMEM(table.shape, jnp.int32),
            pltpu.SemaphoreType.DMA,
        ],
        compiler_params=pltpu.CompilerParams(vmem_limit_bytes=48 << 20),
        cost_estimate=pl.CostEstimate(flops=2 * macs, bytes_accessed=1 << 20, transcendentals=0),
    )(me, table, *blocks)


def on_device(data, bank, select, shifts):
    channels, samples = data.shape
    templates = select.shape[0]
    held = bank.shape[0]
    count = lax.axis_size("tm")
    stations = lax.axis_size("sta")
    me = lax.axis_index("tm")
    seg_rows = samples // LANES
    per = -(-channels // count)
    spare = per * count - channels
    if spare:
        data = jnp.pad(data, ((0, spare), (0, 0)))
        bank = jnp.pad(bank, ((0, 0), (0, spare), (0, 0)))
        shifts = jnp.pad(shifts, ((0, 0), (0, spare)))

    packed = pack(me.reshape(1), select, shifts, data, bank, count)
    blocks, table = list(packed[:count]), packed[count]
    order = visiting_order(count)
    blocks = blocks[:1] + [exchange(blocks[step], "tm", step) for step in order]
    stacks = correlate(blocks, order, me.reshape(1), table, templates, per, held, seg_rows)

    mine = lax.axis_index("sta")
    stacks = stacks.reshape(stations, templates // stations, seg_rows * count, LANES)
    summed = lax.dynamic_index_in_dim(stacks, mine, 0, keepdims=False)
    for step in range(1, stations):
        there = lax.rem(mine + step, stations)
        part = lax.dynamic_index_in_dim(stacks, there, 0, keepdims=False)
        summed = summed + passed_on(part, "sta", step)
    parts, step = [summed], 1
    while step < count:
        radix = 2 if (count // step).bit_length() % 2 == 0 else 4
        summed = functools.reduce(jnp.add, parts)
        parts = [summed] + [exchange(summed, "tm", step * turn) for turn in reversed(range(1, radix))]
        step *= radix
    return finish(parts, me.reshape(1), seg_rows)


def solution(mesh):
    in_specs = (P("sta", "tm"), P("tm", "sta", None), P(), P(None, "sta"))
    out_specs = P("sta", "tm")
    return jax.shard_map(
        on_device, mesh=mesh, in_specs=in_specs, out_specs=out_specs, check_vma=False
    )
```

```python
import functools

import jax
import jax.numpy as jnp
from jax import lax
from jax.experimental import pallas as pl
from jax.experimental.pallas import tpu as pltpu
from jax.sharding import PartitionSpec as P

TL = 1024
MAXSHIFT = 256
LANES = 128
TPL_ROWS = TL // LANES
SHIFT_ROWS = MAXSHIFT // LANES
GROUP = 8
BEYOND = SHIFT_ROWS + TPL_ROWS + 1
CHUNKS = TPL_ROWS + 1
LAG_ROWS = 8
HALF = LANES // 2
PACK_VMEM = 24 << 20


def exchange(value, axis, step):
    count = lax.axis_size(axis)
    return lax.ppermute(value, axis, [(i, i ^ step) for i in range(count)])


def visiting_order(count):
    half = max(count // 2, 1)
    far, near = range(count - 1, half - 1, -1), range(half - 1, 0, -1)
    order = [step for part in (far, near) for odd in (1, 0) for step in part if step % 2 == odd]
    return order


def passed_on(value, axis, step):
    count = lax.axis_size(axis)
    return lax.ppermute(value, axis, [(i, (i + step) % count) for i in range(count)])


def pack_kernel(dims, me_ref, select_hbm, shifts_hbm, data_hbm, bank_hbm, *refs):
    count, per, held, seg_rows, templates = dims
    blocks, table_ref = refs[:count], refs[count]
    select_ref, shifts_ref, data_ref, bank_ref, wave_ref, tpl_ref, sems = refs[count + 1 :]
    pairs = [
        (bank_hbm, bank_ref),
        (data_hbm, data_ref),
        (select_hbm, select_ref),
        (shifts_hbm, shifts_ref),
    ]
    fetch = [pltpu.make_async_copy(a, b, sems.at[i]) for i, (a, b) in enumerate(pairs)]
    for copy in fetch:
        copy.start()
    me = me_ref[0]
    fetch[0].wait()
    for e in range(held):
        for q in range(TPL_ROWS):
            piece = bank_ref[e, :, pl.ds(q * LANES, LANES)].astype(jnp.float32)
            tpl_ref[pl.ds(q, count * per, stride=TPL_ROWS), :] = piece
        for i in range(count):
            start = pl.multiple_of((me ^ i) * (per * TPL_ROWS), TPL_ROWS)
            part = tpl_ref[pl.ds(start, per * TPL_ROWS), :]
            place = pl.ds(per * seg_rows + e * per * TPL_ROWS, per * TPL_ROWS)
            blocks[i][place, :] = part.astype(jnp.bfloat16)
    fetch[1].wait()
    for r in range(seg_rows):
        piece = data_ref[:, pl.ds(r * LANES, LANES)].astype(jnp.float32)
        wave_ref[pl.ds(r, count * per, stride=seg_rows), :] = piece
    for i in range(count):
        start = pl.multiple_of((me ^ i) * (per * seg_rows), 8)
        part = wave_ref[pl.ds(start, per * seg_rows), :]
        blocks[i][pl.ds(0, per * seg_rows), :] = part.astype(jnp.bfloat16)
    fetch[2].wait()
    fetch[3].wait()
    for k in range(templates):
        table_ref[k] = select_ref[k]
        for c in range(per):
            table_ref[templates * (c + 1) + k] = shifts_ref[k, me * per + c]


def pack(me, select, shifts, data, bank, count):
    channels, samples = data.shape
    held = bank.shape[0]
    per, seg_rows = channels // count, samples // LANES
    hbm = pl.BlockSpec(memory_space=pltpu.MemorySpace.HBM)
    vmem = pl.BlockSpec(memory_space=pltpu.VMEM)
    smem = pl.BlockSpec(memory_space=pltpu.SMEM)
    templates = select.shape[0]
    block = jax.ShapeDtypeStruct((per * (seg_rows + held * TPL_ROWS), LANES), jnp.bfloat16)
    return pl.pallas_call(
        functools.partial(pack_kernel, (count, per, held, seg_rows, templates)),
        out_shape=[block] * count + [jax.ShapeDtypeStruct((templates * (per + 1),), jnp.int32)],
        in_specs=[smem] + [hbm] * 4,
        out_specs=[vmem] * count + [smem],
        scratch_shapes=[
            pltpu.SMEM(select.shape, jnp.int32),
            pltpu.SMEM(shifts.shape, jnp.int32),
            pltpu.VMEM(data.shape, jnp.bfloat16),
            pltpu.VMEM(bank.shape, jnp.bfloat16),
            pltpu.VMEM((channels * seg_rows, LANES), jnp.float32),
            pltpu.VMEM((channels * TPL_ROWS, LANES), jnp.float32),
            pltpu.SemaphoreType.DMA((4,)),
        ],
        compiler_params=pltpu.CompilerParams(vmem_limit_bytes=PACK_VMEM),
    )(me, *[pltpu.with_memory_space_constraint(v, pltpu.MemorySpace.HBM) for v in (select, shifts, data, bank)])


def finish_kernel(seg_rows, me_ref, *refs):
    parts, out_ref = refs[:-1], refs[-1]
    me = me_ref[0]
    start = (me // GROUP) * (seg_rows * GROUP) + me % GROUP
    for j in range(out_ref.shape[0]):
        total = functools.reduce(jnp.add, [part[j] for part in parts])
        peak = jnp.max(jnp.max(jnp.abs(total), 0, keepdims=True), 1, keepdims=True)
        rows = [part[j, pl.ds(start, seg_rows, stride=GROUP), :] for part in parts]
        segment = functools.reduce(jnp.add, rows) / (peak + 1e-06)
        for r in range(seg_rows):
            out_ref[pl.ds(j, 1), pl.ds(r * LANES, LANES)] = segment[r : r + 1]


def finish(parts, me, seg_rows):
    smem = pl.BlockSpec(memory_space=pltpu.SMEM)
    vmem = pl.BlockSpec(memory_space=pltpu.VMEM)
    return pl.pallas_call(
        functools.partial(finish_kernel, seg_rows),
        out_shape=jax.ShapeDtypeStruct((parts[0].shape[0], seg_rows * LANES), jnp.float32),
        in_specs=[smem] + [vmem] * len(parts),
        out_specs=vmem,
        compiler_params=pltpu.CompilerParams(vmem_limit_bytes=24 << 20),
    )(me, *parts)


def correlate_kernel(dims, steps, me_ref, table_vmem, *refs):
    count, per, held, seg_rows, templates = dims
    blocks = refs[:count]
    out_ref, rows_ref, bank_ref, norm_ref, lag_a, lag_b, *more = refs[count:]
    lag_c, win_a, win_b, win_c, late_a, late_b, late_c, raw_a, raw_b, raw_c, table_ref, sem = more
    fetch = pltpu.make_async_copy(table_vmem, table_ref, sem)
    fetch.start()
    groups = count // GROUP
    tiles = seg_rows + BEYOND
    block_rows = seg_rows * GROUP
    starts = (seg_rows + SHIFT_ROWS) * GROUP
    paired = starts + (TPL_ROWS - 1) * GROUP
    me = me_ref[0]
    data_rows = per * seg_rows
    bank_rows = per * TPL_ROWS

    for block, step in zip(blocks, steps):
        source = me ^ step
        before = lax.rem(source - 1 + count, count)
        part = block[pl.ds(0, data_rows), :].astype(jnp.float32)
        for c in range(per):
            piece = part[c * seg_rows : (c + 1) * seg_rows]
            at = (c * groups + source // GROUP) * (tiles * GROUP) + source % GROUP
            rows_ref[pl.ds(at, seg_rows, stride=GROUP), :] = piece
            piece = jnp.where(source > 0, piece[:BEYOND], 0.0)
            at = (c * groups + before // GROUP) * (tiles * GROUP) + before % GROUP
            rows_ref[pl.ds(at + block_rows, BEYOND, stride=GROUP), :] = piece
        part = block[pl.ds(data_rows, held * bank_rows), :].astype(jnp.float32)
        bank_ref[pl.ds(source * held, held)] = part.reshape(held, bank_rows, LANES)

    fetch.wait()

    chosen = jnp.concatenate([bank_ref[pl.ds(table_ref[k], 1)] for k in range(templates)], 0)
    chosen = chosen.reshape(templates, per, TPL_ROWS, LANES)
    mean = jnp.sum(jnp.sum(chosen, 2, keepdims=True), 3, keepdims=True) * (1.0 / TL)
    centred = chosen - mean
    power = jnp.sum(jnp.sum(centred * centred, 2, keepdims=True), 3, keepdims=True)
    normed = centred * lax.rsqrt(power + 1e-05)
    norm_ref[...] = normed.astype(jnp.bfloat16).astype(jnp.float32)

    lane = lax.broadcasted_iota(jnp.int32, (LANES, 2 * LANES), 1)
    depth = lax.broadcasted_iota(jnp.int32, (LANES, 2 * LANES), 0)
    summing = jnp.where(lane <= depth, 1.0, jnp.where(lane >= LANES, 1.0, 0.0)).astype(jnp.bfloat16)
    summing_twice = jnp.concatenate([summing, summing], 0)

    def window(values, weights):
        got = jnp.dot(values, weights, preferred_element_type=jnp.float32)
        tail, total = got[:, :LANES], got[:, LANES:]
        for reach in (1, 2, 4):
            extent = total.shape[0] - reach * GROUP
            total = total[:extent] + total[reach * GROUP :]
        far = TPL_ROWS * GROUP
        return tail[:starts] - tail[far : far + starts] + total[GROUP : GROUP + starts]

    step_lane = lax.broadcasted_iota(jnp.int32, (LAG_ROWS, LANES), 1)
    step_row = lax.broadcasted_iota(jnp.int32, (LAG_ROWS, LANES), 0)

    def prepare(c, lag_ref, which):
        for k in which:
            spread = [
                jnp.broadcast_to(norm_ref[k, c, pl.ds(p, 1), :], (LAG_ROWS, LANES))
                for p in range(TPL_ROWS)
            ]
            for group in range(HALF // LAG_ROWS):
                ahead = step_lane >= step_row + group * LAG_ROWS
                turned = [
                    pltpu.roll(row, group * LAG_ROWS, 1, stride=1, stride_axis=0) for row in spread
                ]
                zero = jnp.zeros((LAG_ROWS, LANES), jnp.float32)
                pieces = [
                    jnp.where(ahead, now, old) for now, old in zip(turned + [zero], [zero] + turned)
                ]
                place = pl.ds(k * HALF + group * LAG_ROWS, LAG_ROWS)
                lag_ref[place, :] = jnp.concatenate(pieces, 1).astype(jnp.bfloat16)

    def accumulate(c, first, lag_ref, win_ref, late_ref, raw_ref):
        def group(g):
            base = pl.multiple_of((c * groups + g) * (tiles * GROUP), GROUP)
            series = rows_ref[pl.ds(base, tiles * GROUP), :]

            heard = series[: starts + TPL_ROWS * GROUP]
            squared = heard * heard
            high = squared.astype(jnp.bfloat16)
            low = (squared - high.astype(jnp.float32)).astype(jnp.bfloat16)
            window_sum = window(heard.astype(jnp.bfloat16), summing)
            window_sq = window(jnp.concatenate([high, low], 1), summing_twice)
            spread = window_sq - window_sum * window_sum * (1.0 / TL)
            scale = lax.rsqrt(jnp.maximum(spread, TL / 8.0))

            extent = paired + GROUP
            latter = lax.broadcasted_iota(jnp.int32, (extent, LANES), 1) >= HALF
            later = jnp.where(latter, series[:extent], series[GROUP : GROUP + extent])
            later = pltpu.roll(later, HALF, 1)
            for ref, values in ((win_ref, series), (late_ref, later)):
                both = [values[:paired], values[GROUP : GROUP + paired]]
                ref[...] = jnp.concatenate(both, 1).astype(jnp.bfloat16)

            def windows(ref):
                pieces = [ref[pl.ds(q * GROUP, starts), :] for q in range(0, TPL_ROWS, 2)]
                pieces.append(ref[pl.ds(paired - starts, starts), pl.ds(LANES, LANES)])
                return jnp.concatenate(pieces, 1)

            raw = lax.dot_general(
                jnp.concatenate([windows(win_ref), windows(late_ref)], 0),
                lag_ref[...],
                (((1,), (1,)), ((), ())),
                preferred_element_type=jnp.float32,
            )
            latter = lax.broadcasted_iota(jnp.int32, (starts, LANES), 1) >= HALF
            for k in range(0, templates, 2):
                early = raw[:starts, k * HALF : k * HALF + LANES]
                late = raw[starts:, k * HALF : k * HALF + LANES]
                kept = jnp.where(latter, late, early)
                swapped = pltpu.roll(jnp.where(latter, early, late), HALF, 1)
                raw_ref[k] = jnp.where(latter, swapped, kept) * scale
                raw_ref[k + 1] = jnp.where(latter, kept, swapped) * scale
            lanes = lax.broadcasted_iota(jnp.int32, (block_rows, LANES), 1)
            for k in range(templates):
                shift = table_ref[templates * (c + 1) + k]
                whole, part = shift // LANES, shift % LANES
                at = pl.multiple_of(whole * GROUP, GROUP)
                here = raw_ref[k, pl.ds(at, block_rows), :]
                after = raw_ref[k, pl.ds(at + GROUP, block_rows), :]
                moved = pltpu.roll(jnp.where(lanes >= part, here, after), LANES - part, 1)
                place = pl.ds(pl.multiple_of(g * block_rows, block_rows), block_rows)
                if first:
                    out_ref[k, place, :] = moved
                else:
                    out_ref[k, place, :] += moved

        if groups == 1:
            group(0)
        else:
            pl.loop(0, groups)(group)

    buffers = [(lag_a, win_a, late_a, raw_a), (lag_b, win_b, late_b, raw_b), (lag_c, win_c, late_c, raw_c)]
    prepare(0, lag_a, range(templates))
    for c in range(per):
        following = buffers[(c + 1) % 3][0]
        if c + 1 < per:
            prepare(c + 1, following, range(0, templates // 2))
        accumulate(c, c == 0, *buffers[c % 3])
        if c + 1 < per:
            prepare(c + 1, following, range(templates // 2, templates))


def correlate(blocks, order, me, table, templates, per, held, seg_rows):
    count = len(blocks)
    rows = seg_rows * count
    starts = (seg_rows + SHIFT_ROWS) * GROUP
    paired = starts + (TPL_ROWS - 1) * GROUP
    smem = pl.BlockSpec(memory_space=pltpu.SMEM)
    vmem = pl.BlockSpec(memory_space=pltpu.VMEM)
    f32, bf16 = jnp.float32, jnp.bfloat16
    macs = per * rows * CHUNKS * LANES * templates * LANES
    return pl.pallas_call(
        functools.partial(correlate_kernel, (count, per, held, seg_rows, templates), [0] + order),
        out_shape=jax.ShapeDtypeStruct((templates, rows, LANES), f32),
        in_specs=[smem, vmem] + [vmem] * count,
        out_specs=vmem,
        scratch_shapes=[
            pltpu.VMEM((per * count * (seg_rows + BEYOND) + GROUP * GROUP, LANES), f32),
            pltpu.VMEM((count * held, per * TPL_ROWS, LANES), f32),
            pltpu.VMEM((templates, per, TPL_ROWS, LANES), f32),
            *[pltpu.VMEM((templates * HALF, CHUNKS * LANES), bf16)] * 3,
            *[pltpu.VMEM((paired, 2 * LANES), bf16)] * 6,
            *[pltpu.VMEM((templates, starts, LANES), f32)] * 3,
            pltpu.SMEM(table.shape, jnp.int32),
            pltpu.SemaphoreType.DMA,
        ],
        compiler_params=pltpu.CompilerParams(vmem_limit_bytes=48 << 20),
        cost_estimate=pl.CostEstimate(flops=2 * macs, bytes_accessed=1 << 20, transcendentals=0),
    )(me, table, *blocks)


def on_device(data, bank, select, shifts):
    channels, samples = data.shape
    templates = select.shape[0]
    held = bank.shape[0]
    count = lax.axis_size("tm")
    stations = lax.axis_size("sta")
    me = lax.axis_index("tm")
    seg_rows = samples // LANES
    per = -(-channels // count)
    spare = per * count - channels
    if spare:
        data = jnp.pad(data, ((0, spare), (0, 0)))
        bank = jnp.pad(bank, ((0, 0), (0, spare), (0, 0)))
        shifts = jnp.pad(shifts, ((0, 0), (0, spare)))

    packed = pack(me.reshape(1), select, shifts, data, bank, count)
    blocks, table = list(packed[:count]), packed[count]
    order = visiting_order(count)
    blocks = blocks[:1] + [exchange(blocks[step], "tm", step) for step in order]
    stacks = correlate(blocks, order, me.reshape(1), table, templates, per, held, seg_rows)

    mine = lax.axis_index("sta")
    stacks = stacks.reshape(stations, templates // stations, seg_rows * count, LANES)
    summed = lax.dynamic_index_in_dim(stacks, mine, 0, keepdims=False)
    for step in reversed(range(1, stations)):
        there = lax.rem(mine + step, stations)
        part = lax.dynamic_index_in_dim(stacks, there, 0, keepdims=False)
        summed = summed + passed_on(part, "sta", step)
    parts, step = [summed], 1
    while step < count:
        radix = 2 if (count // step).bit_length() % 2 == 0 else 4
        summed = functools.reduce(jnp.add, parts)
        parts = [summed] + [exchange(summed, "tm", step * turn) for turn in reversed(range(1, radix))]
        step *= radix
    return finish(parts, me.reshape(1), seg_rows)


def solution(mesh):
    in_specs = (P("sta", "tm"), P("tm", "sta", None), P(), P(None, "sta"))
    out_specs = P("sta", "tm")
    return jax.shard_map(
        on_device, mesh=mesh, in_specs=in_specs, out_specs=out_specs, check_vma=False
    )
```

```python
import functools

import jax
import jax.numpy as jnp
from jax import lax
from jax.experimental import pallas as pl
from jax.experimental.pallas import tpu as pltpu
from jax.sharding import PartitionSpec as P

TL = 1024
MAXSHIFT = 256
LANES = 128
TPL_ROWS = TL // LANES
SHIFT_ROWS = MAXSHIFT // LANES
GROUP = 8
BEYOND = SHIFT_ROWS + TPL_ROWS + 1
CHUNKS = TPL_ROWS + 1
LAG_ROWS = 8
HALF = LANES // 2
PACK_VMEM = 24 << 20


def exchange(value, axis, step):
    count = lax.axis_size(axis)
    return lax.ppermute(value, axis, [(i, i ^ step) for i in range(count)])


def visiting_order(count):
    half = max(count // 2, 1)
    far, near = range(count - 1, half - 1, -1), range(half - 1, 0, -1)
    order = [step for part in (far, near) for odd in (1, 0) for step in part if step % 2 == odd]
    return order


def passed_on(value, axis, step):
    count = lax.axis_size(axis)
    return lax.ppermute(value, axis, [(i, (i + step) % count) for i in range(count)])


def pack_kernel(dims, me_ref, select_hbm, shifts_hbm, data_hbm, bank_hbm, *refs):
    count, per, held, seg_rows, templates = dims
    blocks, table_ref = refs[:count], refs[count]
    select_ref, shifts_ref, data_ref, bank_ref, wave_ref, tpl_ref, sems = refs[count + 1 :]
    pairs = [
        (bank_hbm, bank_ref),
        (data_hbm, data_ref),
        (select_hbm, select_ref),
        (shifts_hbm, shifts_ref),
    ]
    fetch = [pltpu.make_async_copy(a, b, sems.at[i]) for i, (a, b) in enumerate(pairs)]
    for copy in fetch:
        copy.start()
    me = me_ref[0]
    fetch[0].wait()
    for e in range(held):
        for q in range(TPL_ROWS):
            piece = bank_ref[e, :, pl.ds(q * LANES, LANES)].astype(jnp.float32)
            tpl_ref[pl.ds(q, count * per, stride=TPL_ROWS), :] = piece
        for i in range(count):
            start = pl.multiple_of((me ^ i) * (per * TPL_ROWS), TPL_ROWS)
            part = tpl_ref[pl.ds(start, per * TPL_ROWS), :]
            place = pl.ds(per * seg_rows + e * per * TPL_ROWS, per * TPL_ROWS)
            blocks[i][place, :] = part.astype(jnp.bfloat16)
    fetch[1].wait()
    for r in range(seg_rows):
        piece = data_ref[:, pl.ds(r * LANES, LANES)].astype(jnp.float32)
        wave_ref[pl.ds(r, count * per, stride=seg_rows), :] = piece
    for i in range(count):
        start = pl.multiple_of((me ^ i) * (per * seg_rows), 8)
        part = wave_ref[pl.ds(start, per * seg_rows), :]
        blocks[i][pl.ds(0, per * seg_rows), :] = part.astype(jnp.bfloat16)
    fetch[2].wait()
    fetch[3].wait()
    for k in range(templates):
        table_ref[k] = select_ref[k]
        for c in range(per):
            table_ref[templates * (c + 1) + k] = shifts_ref[k, me * per + c]


def pack(me, select, shifts, data, bank, count):
    channels, samples = data.shape
    held = bank.shape[0]
    per, seg_rows = channels // count, samples // LANES
    hbm = pl.BlockSpec(memory_space=pltpu.MemorySpace.HBM)
    vmem = pl.BlockSpec(memory_space=pltpu.VMEM)
    smem = pl.BlockSpec(memory_space=pltpu.SMEM)
    templates = select.shape[0]
    block = jax.ShapeDtypeStruct((per * (seg_rows + held * TPL_ROWS), LANES), jnp.bfloat16)
    return pl.pallas_call(
        functools.partial(pack_kernel, (count, per, held, seg_rows, templates)),
        out_shape=[block] * count + [jax.ShapeDtypeStruct((templates * (per + 1),), jnp.int32)],
        in_specs=[smem] + [hbm] * 4,
        out_specs=[vmem] * count + [smem],
        scratch_shapes=[
            pltpu.SMEM(select.shape, jnp.int32),
            pltpu.SMEM(shifts.shape, jnp.int32),
            pltpu.VMEM(data.shape, jnp.bfloat16),
            pltpu.VMEM(bank.shape, jnp.bfloat16),
            pltpu.VMEM((channels * seg_rows, LANES), jnp.float32),
            pltpu.VMEM((channels * TPL_ROWS, LANES), jnp.float32),
            pltpu.SemaphoreType.DMA((4,)),
        ],
        compiler_params=pltpu.CompilerParams(vmem_limit_bytes=PACK_VMEM),
    )(me, *[pltpu.with_memory_space_constraint(v, pltpu.MemorySpace.HBM) for v in (select, shifts, data, bank)])


def finish_kernel(seg_rows, me_ref, *refs):
    parts, out_ref = refs[:-1], refs[-1]
    me = me_ref[0]
    start = (me // GROUP) * (seg_rows * GROUP) + me % GROUP
    for j in range(out_ref.shape[0]):
        total = functools.reduce(jnp.add, [part[j] for part in parts])
        peak = jnp.max(jnp.max(jnp.abs(total), 0, keepdims=True), 1, keepdims=True)
        rows = [part[j, pl.ds(start, seg_rows, stride=GROUP), :] for part in parts]
        segment = functools.reduce(jnp.add, rows) / (peak + 1e-06)
        for r in range(seg_rows):
            out_ref[pl.ds(j, 1), pl.ds(r * LANES, LANES)] = segment[r : r + 1]


def finish(parts, me, seg_rows):
    smem = pl.BlockSpec(memory_space=pltpu.SMEM)
    vmem = pl.BlockSpec(memory_space=pltpu.VMEM)
    return pl.pallas_call(
        functools.partial(finish_kernel, seg_rows),
        out_shape=jax.ShapeDtypeStruct((parts[0].shape[0], seg_rows * LANES), jnp.float32),
        in_specs=[smem] + [vmem] * len(parts),
        out_specs=vmem,
        compiler_params=pltpu.CompilerParams(vmem_limit_bytes=24 << 20),
    )(me, *parts)


def correlate_kernel(dims, steps, me_ref, table_vmem, *refs):
    count, per, held, seg_rows, templates = dims
    blocks = refs[:count]
    out_ref, rows_ref, bank_ref, norm_ref, lag_a, lag_b, *more = refs[count:]
    lag_c, win_a, win_b, win_c, late_a, late_b, late_c, raw_a, raw_b, raw_c, table_ref, sem = more
    fetch = pltpu.make_async_copy(table_vmem, table_ref, sem)
    fetch.start()
    groups = count // GROUP
    tiles = seg_rows + BEYOND
    block_rows = seg_rows * GROUP
    starts = (seg_rows + SHIFT_ROWS) * GROUP
    paired = starts + (TPL_ROWS - 1) * GROUP
    me = me_ref[0]
    data_rows = per * seg_rows
    bank_rows = per * TPL_ROWS

    for block, step in zip(blocks, steps):
        source = me ^ step
        before = lax.rem(source - 1 + count, count)
        part = block[pl.ds(0, data_rows), :].astype(jnp.float32)
        for c in range(per):
            piece = part[c * seg_rows : (c + 1) * seg_rows]
            at = (c * groups + source // GROUP) * (tiles * GROUP) + source % GROUP
            rows_ref[pl.ds(at, seg_rows, stride=GROUP), :] = piece
            piece = jnp.where(source > 0, piece[:BEYOND], 0.0)
            at = (c * groups + before // GROUP) * (tiles * GROUP) + before % GROUP
            rows_ref[pl.ds(at + block_rows, BEYOND, stride=GROUP), :] = piece
        part = block[pl.ds(data_rows, held * bank_rows), :].astype(jnp.float32)
        bank_ref[pl.ds(source * held, held)] = part.reshape(held, bank_rows, LANES)

    fetch.wait()

    chosen = jnp.concatenate([bank_ref[pl.ds(table_ref[k], 1)] for k in range(templates)], 0)
    chosen = chosen.reshape(templates, per, TPL_ROWS, LANES)
    mean = jnp.sum(jnp.sum(chosen, 2, keepdims=True), 3, keepdims=True) * (1.0 / TL)
    centred = chosen - mean
    power = jnp.sum(jnp.sum(centred * centred, 2, keepdims=True), 3, keepdims=True)
    normed = centred * lax.rsqrt(power + 1e-05)
    norm_ref[...] = normed.astype(jnp.bfloat16).astype(jnp.float32)

    lane = lax.broadcasted_iota(jnp.int32, (LANES, 2 * LANES), 1)
    depth = lax.broadcasted_iota(jnp.int32, (LANES, 2 * LANES), 0)
    summing = jnp.where(lane <= depth, 1.0, jnp.where(lane >= LANES, 1.0, 0.0)).astype(jnp.bfloat16)
    summing_twice = jnp.concatenate([summing, summing], 0)

    def window(values, weights):
        got = jnp.dot(values, weights, preferred_element_type=jnp.float32)
        tail, total = got[:, :LANES], got[:, LANES:]
        for reach in (1, 2, 4):
            extent = total.shape[0] - reach * GROUP
            total = total[:extent] + total[reach * GROUP :]
        far = TPL_ROWS * GROUP
        return tail[:starts] - tail[far : far + starts] + total[GROUP : GROUP + starts]

    step_lane = lax.broadcasted_iota(jnp.int32, (LAG_ROWS, LANES), 1)
    step_row = lax.broadcasted_iota(jnp.int32, (LAG_ROWS, LANES), 0)

    def prepare(c, lag_ref, which):
        for k in which:
            spread = [
                jnp.broadcast_to(norm_ref[k, c, pl.ds(p, 1), :], (LAG_ROWS, LANES))
                for p in range(TPL_ROWS)
            ]
            for group in range(HALF // LAG_ROWS):
                ahead = step_lane >= step_row + group * LAG_ROWS
                turned = [
                    pltpu.roll(row, group * LAG_ROWS, 1, stride=1, stride_axis=0) for row in spread
                ]
                zero = jnp.zeros((LAG_ROWS, LANES), jnp.float32)
                pieces = [
                    jnp.where(ahead, now, old) for now, old in zip(turned + [zero], [zero] + turned)
                ]
                place = pl.ds(k * HALF + group * LAG_ROWS, LAG_ROWS)
                lag_ref[place, :] = jnp.concatenate(pieces, 1).astype(jnp.bfloat16)

    def accumulate(c, first, beside, lag_ref, win_ref, late_ref, raw_ref):
        def group(g):
            base = pl.multiple_of((c * groups + g) * (tiles * GROUP), GROUP)
            series = rows_ref[pl.ds(base, tiles * GROUP), :]

            heard = series[: starts + TPL_ROWS * GROUP]
            squared = heard * heard
            high = squared.astype(jnp.bfloat16)
            low = (squared - high.astype(jnp.float32)).astype(jnp.bfloat16)
            window_sum = window(heard.astype(jnp.bfloat16), summing)
            window_sq = window(jnp.concatenate([high, low], 1), summing_twice)
            spread = window_sq - window_sum * window_sum * (1.0 / TL)
            scale = lax.rsqrt(jnp.maximum(spread, TL / 8.0))

            extent = paired + GROUP
            latter = lax.broadcasted_iota(jnp.int32, (extent, LANES), 1) >= HALF
            later = jnp.where(latter, series[:extent], series[GROUP : GROUP + extent])
            later = pltpu.roll(later, HALF, 1)
            for ref, values in ((win_ref, series), (late_ref, later)):
                both = [values[:paired], values[GROUP : GROUP + paired]]
                ref[...] = jnp.concatenate(both, 1).astype(jnp.bfloat16)

            def windows(ref):
                pieces = [ref[pl.ds(q * GROUP, starts), :] for q in range(0, TPL_ROWS, 2)]
                pieces.append(ref[pl.ds(paired - starts, starts), pl.ds(LANES, LANES)])
                return jnp.concatenate(pieces, 1)

            raw = lax.dot_general(
                jnp.concatenate([windows(win_ref), windows(late_ref)], 0),
                lag_ref[...],
                (((1,), (1,)), ((), ())),
                preferred_element_type=jnp.float32,
            )
            latter = lax.broadcasted_iota(jnp.int32, (starts, LANES), 1) >= HALF
            for k in range(0, templates, 2):
                early = raw[:starts, k * HALF : k * HALF + LANES]
                late = raw[starts:, k * HALF : k * HALF + LANES]
                kept = jnp.where(latter, late, early)
                swapped = pltpu.roll(jnp.where(latter, early, late), HALF, 1)
                raw_ref[k] = jnp.where(latter, swapped, kept) * scale
                raw_ref[k + 1] = jnp.where(latter, kept, swapped) * scale
            if groups == 1:
                beside()
            lanes = lax.broadcasted_iota(jnp.int32, (block_rows, LANES), 1)
            for k in range(templates):
                shift = table_ref[templates * (c + 1) + k]
                whole, part = shift // LANES, shift % LANES
                at = pl.multiple_of(whole * GROUP, GROUP)
                here = raw_ref[k, pl.ds(at, block_rows), :]
                after = raw_ref[k, pl.ds(at + GROUP, block_rows), :]
                moved = pltpu.roll(jnp.where(lanes >= part, here, after), LANES - part, 1)
                place = pl.ds(pl.multiple_of(g * block_rows, block_rows), block_rows)
                if first:
                    out_ref[k, place, :] = moved
                else:
                    out_ref[k, place, :] += moved

        if groups == 1:
            group(0)
        else:
            beside()
            pl.loop(0, groups)(group)

    buffers = [(lag_a, win_a, late_a, raw_a), (lag_b, win_b, late_b, raw_b), (lag_c, win_c, late_c, raw_c)]
    prepare(0, lag_a, range(templates))
    for c in range(per):
        following = buffers[(c + 1) % 3][0]

        def beside():
            if c + 1 < per:
                prepare(c + 1, following, range(templates // 2, templates))

        if c + 1 < per:
            prepare(c + 1, following, range(0, templates // 2))
        accumulate(c, c == 0, beside, *buffers[c % 3])


def correlate(blocks, order, me, table, templates, per, held, seg_rows):
    count = len(blocks)
    rows = seg_rows * count
    starts = (seg_rows + SHIFT_ROWS) * GROUP
    paired = starts + (TPL_ROWS - 1) * GROUP
    smem = pl.BlockSpec(memory_space=pltpu.SMEM)
    vmem = pl.BlockSpec(memory_space=pltpu.VMEM)
    f32, bf16 = jnp.float32, jnp.bfloat16
    macs = per * rows * CHUNKS * LANES * templates * LANES
    return pl.pallas_call(
        functools.partial(correlate_kernel, (count, per, held, seg_rows, templates), [0] + order),
        out_shape=jax.ShapeDtypeStruct((templates, rows, LANES), f32),
        in_specs=[smem, vmem] + [vmem] * count,
        out_specs=vmem,
        scratch_shapes=[
            pltpu.VMEM((per * count * (seg_rows + BEYOND) + GROUP * GROUP, LANES), f32),
            pltpu.VMEM((count * held, per * TPL_ROWS, LANES), f32),
            pltpu.VMEM((templates, per, TPL_ROWS, LANES), f32),
            *[pltpu.VMEM((templates * HALF, CHUNKS * LANES), bf16)] * 3,
            *[pltpu.VMEM((paired, 2 * LANES), bf16)] * 6,
            *[pltpu.VMEM((templates, starts, LANES), f32)] * 3,
            pltpu.SMEM(table.shape, jnp.int32),
            pltpu.SemaphoreType.DMA,
        ],
        compiler_params=pltpu.CompilerParams(vmem_limit_bytes=48 << 20),
        cost_estimate=pl.CostEstimate(flops=2 * macs, bytes_accessed=1 << 20, transcendentals=0),
    )(me, table, *blocks)


def on_device(data, bank, select, shifts):
    channels, samples = data.shape
    templates = select.shape[0]
    held = bank.shape[0]
    count = lax.axis_size("tm")
    stations = lax.axis_size("sta")
    me = lax.axis_index("tm")
    seg_rows = samples // LANES
    per = -(-channels // count)
    spare = per * count - channels
    if spare:
        data = jnp.pad(data, ((0, spare), (0, 0)))
        bank = jnp.pad(bank, ((0, 0), (0, spare), (0, 0)))
        shifts = jnp.pad(shifts, ((0, 0), (0, spare)))

    packed = pack(me.reshape(1), select, shifts, data, bank, count)
    blocks, table = list(packed[:count]), packed[count]
    order = visiting_order(count)
    blocks = blocks[:1] + [exchange(blocks[step], "tm", step) for step in order]
    stacks = correlate(blocks, order, me.reshape(1), table, templates, per, held, seg_rows)

    mine = lax.axis_index("sta")
    stacks = stacks.reshape(stations, templates // stations, seg_rows * count, LANES)
    summed = lax.dynamic_index_in_dim(stacks, mine, 0, keepdims=False)
    for step in reversed(range(1, stations)):
        there = lax.rem(mine + step, stations)
        part = lax.dynamic_index_in_dim(stacks, there, 0, keepdims=False)
        summed = summed + passed_on(part, "sta", step)
    parts, step = [summed], 1
    while step < count:
        radix = 2 if (count // step).bit_length() % 2 == 0 else 4
        summed = functools.reduce(jnp.add, parts)
        parts = [summed] + [exchange(summed, "tm", step * turn) for turn in reversed(range(1, radix))]
        step *= radix
    return finish(parts, me.reshape(1), seg_rows)


def solution(mesh):
    in_specs = (P("sta", "tm"), P("tm", "sta", None), P(), P(None, "sta"))
    out_specs = P("sta", "tm")
    return jax.shard_map(
        on_device, mesh=mesh, in_specs=in_specs, out_specs=out_specs, check_vma=False
    )
```
